32 devices in a mesh: groups: 2 (over y), edge: 4 (over z), trip: 2 (over x), sub: 2 (over core).
Axes of the slice: x: 2, y: 2, z: 4, core: 2. Of those that a mesh axis runs over, the one named last changes fastest.
Arguments:
- edge_feat: float32 [128, 128, 512], P(('groups', 'edge'), ('trip', 'sub')), parts along dimension 0, may hold values from -6 to 6
- edge_counts: int32 [128], P(('groups', 'edge')), parts along dimension 0, may hold values from 64 to 128
- reverse: int32 [128], P('groups'), parts along dimension 0, may hold values from 0 to 63, as said below
- patterns: int32 [8, 4, 64, 2], P(('groups', 'edge'), ('trip', 'sub')), parts along dimension 0, may hold values from 0 to 15
- trip_count: int32 [8, 4], P(('groups', 'edge'), ('trip', 'sub')), parts along dimension 0, may hold values from 16 to 64, as said below
- coef: float32 [8, 4, 64, 128, 128], P(('groups', 'edge'), ('trip', 'sub')), parts along dimension 0, may hold values from -0.1875 to 0.1875
- down_weight: float32 [3, 512, 256], replicated, may hold values from -0.25 to 0.25
- up_weight: float32 [3, 256, 512], replicated, may hold values from -0.375 to 0.375
- dense_weight: float32 [3, 512, 512], replicated, may hold values from -0.25 to 0.25
Outputs:
- edge_out: float32 [128, 128, 512], P(('groups', 'edge'), ('trip', 'sub')), parts along dimension 0
The draws below stay inside these ranges and needn't reach their ends.
There are 2 independent parts, one for each index of `groups`. The reference program is written for one: setup_inputs(seed, part) draws one part's arguments, and reference() takes and returns one part's arrays. A program takes and returns all parts, laid end to end along the dimension named above; an argument that names none is the same for every part. Nothing has to cross between parts.
Inputs may be any that keep to these rules, and one draw needn't show every extreme that they name: reverse is an involution without fixed points; reverse[c] lies on another index of edge than c; from one index of edge at most 8 clusters have their reverse on one other index, and that many in every draw. `trip_count`: some device has all 64 slots live in every draw.
All inputs are finite; a program needn't handle non-finite values.
Results may differ from the reference program's by a relative error of at most 0.0003.
Values sent between devices are 32-bit elements; how exact they have to be, the bound alone decides.
A program may use at most 128 MiB of HBM per device.

```python
import jax
import jax.numpy as jnp
from jax import lax

DE = 512
FT = 256
BLK = 128
LAYERS = 3
EB = 16
P_SIZE = 64
GRID = 4
TS = 4
CLUSTERS = 64


def draw_reverse(key, part):
    keys = jax.random.split(jax.random.fold_in(key, 11), 2)
    place_perm = jax.random.permutation(keys[0], GRID).astype(jnp.int32)
    inverse_perm = jnp.zeros((GRID,), jnp.int32).at[place_perm].set(jnp.arange(GRID, dtype=jnp.int32))
    rounds = EB // 2
    round_ids = jnp.arange(rounds, dtype=jnp.int32)
    offsets = 2 * (round_ids % (GRID // 2)) + 1
    partner = inverse_perm[(offsets[None, :] - place_perm[:, None]) % GRID]
    slot_keys = jax.random.split(keys[1], GRID)
    slot_perms = jax.vmap(lambda sub_key: jax.random.permutation(sub_key, EB).astype(jnp.int32))(slot_keys)
    even_slot = slot_perms[:, 0::2]
    odd_slot = slot_perms[:, 1::2]
    partner_even = slot_perms[partner, 2 * round_ids[None, :]]
    partner_odd = slot_perms[partner, 2 * round_ids[None, :] + 1]
    values_even = partner * EB + partner_odd
    values_odd = partner * EB + partner_even
    device_ids = jnp.arange(GRID, dtype=jnp.int32)[:, None]
    result = jnp.zeros((GRID, EB), jnp.int32)
    result = result.at[device_ids, even_slot].set(values_even)
    result = result.at[device_ids, odd_slot].set(values_odd)
    return result.reshape(CLUSTERS).astype(jnp.int32)


def draw_edge_counts(key, part):
    keys = jax.random.split(jax.random.fold_in(key, 23), 3)
    counts = jax.random.randint(keys[0], (CLUSTERS,), BLK // 2, BLK + 1).astype(jnp.int32)
    first = jax.random.randint(keys[1], (), 0, CLUSTERS)
    second = (first + 1 + jax.random.randint(keys[2], (), 0, CLUSTERS - 1)) % CLUSTERS
    counts = counts.at[first].set(BLK).at[second].set(BLK // 2)
    return counts.astype(jnp.int32)


def draw_trip_count(key, part):
    keys = jax.random.split(jax.random.fold_in(key, 37), 2)
    counts = jax.random.randint(keys[0], (GRID * TS,), P_SIZE // 4, P_SIZE + 1).astype(jnp.int32)
    chosen = jax.random.randint(keys[1], (), 0, GRID * TS)
    counts = counts.at[chosen].set(P_SIZE)
    return counts.reshape(GRID, TS).astype(jnp.int32)


def touch_ends(values, stream_key, low, largest):
    place = [jax.random.randint(jax.random.fold_in(stream_key, axis), (), 0, length) for axis, length in enumerate(values.shape)]
    main_axis = values.shape.index(max(values.shape))
    beside = place[:main_axis] + [(place[main_axis] + 1) % values.shape[main_axis]] + place[main_axis + 1:]
    return values.at[tuple(place)].set(low).at[tuple(beside)].set(largest)


def shard_levels(rng, shape, pieces, smallest, top_value):
    def one(axis_at, shards_of):
        heights = jax.random.uniform(jax.random.fold_in(jax.random.fold_in(rng, 6), axis_at), (shards_of,), jnp.float32, smallest / len(pieces), top_value / len(pieces))
        return jnp.repeat(jnp.exp(heights), shape[axis_at] // shards_of).reshape((-1,) + (1,) * (len(shape) - axis_at - 1))

    loudness = one(*pieces[0])
    for cut in pieces[1:]:
        loudness = loudness * one(*cut)
    return loudness


def bell_draw(rng, shape, scale, reach, pieces=(), kind=jnp.bfloat16):
    factor_of = shard_levels(rng, shape, pieces, -0.22, 0.18) if pieces else 1.0
    values = jax.random.normal(rng, shape, jnp.float32) * scale * factor_of
    return jnp.minimum(jnp.maximum(values, -reach), reach).astype(kind)


def setup_inputs(seed: int = 0, part: int = 0) -> dict:
    key_of = jax.random.split(jax.random.key(seed), 10)
    part_keys = jax.random.split(jax.random.fold_in(key_of[9], part), 10)
    return {
        "edge_feat": bell_draw(part_keys[0], (CLUSTERS, BLK, DE), 1.0, 6.0, ((0, 4), (1, 4)), jnp.float32),
        "edge_counts": draw_edge_counts(jax.random.fold_in(jax.random.fold_in(key_of[9], part), 71), part),
        "reverse": draw_reverse(jax.random.fold_in(jax.random.fold_in(key_of[9], part), 71), part),
        "patterns": touch_ends(jax.random.randint(part_keys[3], (GRID, TS, P_SIZE, 2), 0, EB), jax.random.fold_in(part_keys[3], 1), 0, EB - 1).astype(jnp.int32),
        "trip_count": draw_trip_count(jax.random.fold_in(jax.random.fold_in(key_of[9], part), 71), part),
        "coef": bell_draw(part_keys[5], (GRID, TS, P_SIZE, BLK, BLK), (BLK * P_SIZE * TS // (2 * EB)) ** -0.5, 0.1875, ((0, 4), (1, 4)), jnp.float32),
        "down_weight": bell_draw(key_of[6], (LAYERS, DE, FT), DE ** -0.5, 0.25, (), jnp.float32),
        "up_weight": bell_draw(key_of[7], (LAYERS, FT, DE), FT ** -0.5, 0.375, (), jnp.float32),
        "dense_weight": bell_draw(key_of[8], (LAYERS, DE, DE), DE ** -0.5, 0.25, (), jnp.float32),
    }


EXACT_PRECISION = lax.Precision.HIGHEST
INV_THREE = 1.0 / 3.0 ** 0.5
INV_TWO = 1.0 / 2.0 ** 0.5


def reference(edge_feat, edge_counts, reverse, patterns, trip_count, coef, down_weight, up_weight, dense_weight):
    row_ids = jnp.arange(BLK, dtype=jnp.int32)
    valid_row_mask = (row_ids[None, :] < edge_counts[:, None]).astype(jnp.float32)[:, :, None]
    edge_features = edge_feat

    def per_group(inputs):
        group_blocks, pattern_list, live_count, coeffs = inputs
        slot_live = (jnp.arange(P_SIZE, dtype=jnp.int32)[None, :] < live_count[:, None]).astype(jnp.float32)
        flat_pattern = pattern_list.reshape(TS * P_SIZE, 2)
        flat_coeffs = coeffs.reshape(TS * P_SIZE, BLK, BLK)
        picked = jnp.take(group_blocks, flat_pattern[:, 1], axis=0)
        products = jnp.einsum('pij,pjf->pif', flat_coeffs, picked, precision=EXACT_PRECISION)
        products = products * slot_live.reshape(TS * P_SIZE)[:, None, None]
        target_hot = (flat_pattern[:, 0][None, :] == jnp.arange(EB, dtype=jnp.int32)[:, None]).astype(jnp.float32)
        return jnp.einsum('tp,pif->tif', target_hot, products, precision=EXACT_PRECISION)

    for current_layer_index in range(LAYERS):
        reduced_features = jnp.einsum('mrv,ve->mre', edge_features, down_weight[current_layer_index], precision=EXACT_PRECISION) * valid_row_mask
        grouped = reduced_features.reshape(GRID, EB, BLK, FT)
        pooled_messages = lax.map(per_group, (grouped, patterns, trip_count, coef)).reshape(CLUSTERS, BLK, FT)
        raised_features = jnp.einsum('dhi,iw->dhw', pooled_messages, up_weight[current_layer_index], precision=EXACT_PRECISION)
        reversed_feat = jnp.take(raised_features, reverse, axis=0)
        merged_features = (edge_features + raised_features + reversed_feat) * INV_THREE
        dense_output = jnp.einsum('weo,oa->wea', merged_features, dense_weight[current_layer_index], precision=EXACT_PRECISION)
        edge_features = (merged_features + jax.nn.silu(dense_output)) * INV_TWO
    return edge_features
```

```python
import functools

import jax
import jax.numpy as jnp
from jax import lax
from jax.experimental import pallas as pl
from jax.experimental.pallas import tpu as pltpu
from jax.sharding import PartitionSpec as P

INV_THREE = 1.0 / 3.0**0.5
INV_TWO = 1.0 / 2.0**0.5
F32, BF16 = jnp.float32, jnp.bfloat16
MESH = pl.DeviceIdType.MESH
CHUNK = 8


def split(x):
    hi = x.astype(BF16)
    return hi, (x - hi.astype(F32)).astype(BF16)


def dot(a, b):
    return jnp.dot(a, b, preferred_element_type=F32)


def mm3(x, w_hi, w_lo):
    rows = x.shape[0]
    hi, lo = split(x)
    both = dot(jnp.concatenate([hi, lo], axis=0), w_hi)
    return both[:rows] + both[rows:] + dot(hi, w_lo)


def kernel(dims, tab, feat_hbm, coef_hbm, down_hbm, up_hbm, dense_hbm, out, *scratch):
    nt, ns, ne, eb, r, cap, slots, layers, blk, ft, de = dims
    nk, ranks, wide = r // CHUNK, nt * ns, ft // 2
    early = nk - 2 if nk > 2 else 0
    zr, scratch = scratch[: 2 * nk], scratch[2 * nk :]
    (coef, down, up, dense, down_h, down_l, up_h, up_l, dense_h, dense_l, c2, x2, run, part, recv1, recv2, agg, zs, gath, mask,
     in_sem, agx_s, agy_s, agp_s, agf_s, ag_r, r1_s, r1_r, r2_s, r2_r, z_s, z_r, z_free) = scratch
    o_perm, o_src, o_same = 0, slots, 2 * slots
    o_last, o_has = 3 * slots, 3 * slots + eb
    o_zsrc = o_has + eb
    o_zpos = o_zsrc + ne * cap
    o_count = o_zpos + eb
    a, b, e = lax.axis_index("trip"), lax.axis_index("sub"), lax.axis_index("edge")
    other = lax.rem(b + 1, ns)
    me = a * ns + b

    rest = pl.ds(1, layers - 1)
    loads = [
        pltpu.make_async_copy(s, d, in_sem.at[i])
        for i, (s, d) in enumerate(((feat_hbm, out), (down_hbm.at[rest], down.at[rest]), (coef_hbm, coef), (up_hbm, up), (dense_hbm, dense), (down_hbm.at[0], down.at[0])))
    ]
    loads[5].start()
    loads[0].start()

    barrier = pltpu.get_barrier_semaphore()
    for o in range(1, nt):
        for s in (b, other):
            pl.semaphore_signal(barrier, inc=1, device_id={"trip": lax.rem(a + o, nt), "sub": s}, device_id_type=MESH)
    pl.semaphore_signal(barrier, inc=1, device_id={"sub": other}, device_id_type=MESH)
    for o in range(1, ne):
        pl.semaphore_signal(barrier, inc=1, device_id={"edge": lax.rem(e + o, ne)}, device_id_type=MESH)

    def rows(k):
        return pl.ds(k * CHUNK, CHUNK)

    def cols(h):
        return pl.ds(h * wide, wide)

    def remote(src, dst, send, recv, where):
        return pltpu.make_async_remote_copy(
            src_ref=src, dst_ref=dst, send_sem=send, recv_sem=recv, device_id=where, device_id_type=MESH
        )

    def trip(o):
        return lax.rem(a + o, nt)

    def both_cores(k, h):
        return False

    def gather_piece(rank, k, h):
        return gath.at[rank, :, rows(k), cols(h)]

    def ag_far(k, h, o):
        g = gather_piece(me, k, h)
        return remote(g, g, agx_s.at[2 * k + h, o], ag_r.at[2 * k + h, me], {"trip": trip(o), "sub": other})

    def ag_near(k, h, o):
        g = gather_piece(me, k, h)
        return remote(g, g, agy_s.at[2 * k + h, o], ag_r.at[2 * k + h, me], {"trip": trip(o), "sub": b})

    def ag_pair(k, h):
        g = gather_piece(me, k, h)
        return remote(g, g, agp_s.at[2 * k + h], ag_r.at[2 * k + h, me], {"sub": other})

    def ag_forward(k, h, o):
        rank = trip(o) * ns + other
        g = gather_piece(rank, k, h)
        return remote(g, g, agf_s.at[2 * k + h, o], ag_r.at[2 * k + h, rank], {"sub": other})

    def ag_arrive(k, h, rank):
        g = gather_piece(rank, k, h)
        remote(g, g, agp_s.at[2 * k + h], ag_r.at[2 * k + h, rank], {"sub": other}).wait_recv()

    def ag_send(k, h):
        for o in range(1, nt):
            ag_far(k, h, o).start()
            if both_cores(k, h):
                ag_near(k, h, o).start()
        ag_pair(k, h).start()

    def pass_on(k, h):
        for o in range(1, nt):
            ag_arrive(k, h, trip(o) * ns + other)
            if not both_cores(k, h):
                ag_forward(k, h, o).start()

    def ag_finish(h):
        for k in range(nk):
            ag_pair(k, h).wait_send()
            for o in range(1, nt):
                ag_far(k, h, o).wait_send()
                if both_cores(k, h):
                    ag_near(k, h, o).wait_send()
                else:
                    ag_forward(k, h, o).wait_send()

    def rs_pair(k, h):
        return remote(
            part.at[1, :, :, rows(k), cols(h)],
            recv1.at[:, :, rows(k), cols(h)],
            r1_s.at[2 * k + h],
            r1_r.at[2 * k + h],
            {"sub": other},
        )

    def rs_cross(k, h, o):
        return remote(
            part.at[0, o, :, rows(k), cols(h)],
            recv2.at[a, :, rows(k), cols(h)],
            r2_s.at[2 * k + h, o],
            r2_r.at[2 * k + h, a],
            {"trip": trip(o), "sub": other},
        )

    def rs_arrive(k, h, o):
        src = trip(o)
        dst = recv2.at[src, :, rows(k), cols(h)]
        remote(dst, dst, r2_s.at[2 * k + h, o], r2_r.at[2 * k + h, src], {"trip": src, "sub": other}).wait_recv()

    def z_copy(k, h, o):
        peer = lax.rem(e + o, ne)
        return remote(
            zs.at[pl.ds(peer * cap, cap), rows(k), cols(h)],
            zr[2 * k + h].at[pl.ds(e * cap, cap)],
            z_s.at[2 * k + h, o],
            z_r.at[2 * k + h, e],
            {"edge": peer},
        )

    def z_arrive(k, h, o):
        src = lax.rem(e + o, ne)
        dst = zr[2 * k + h].at[pl.ds(src * cap, cap)]
        remote(dst, dst, z_s.at[2 * k + h, o], z_r.at[2 * k + h, src], {"edge": src}).wait_recv()

    def lower(k, layer):
        f = out[:, rows(k), :].reshape(eb * CHUNK, de)
        live = jnp.concatenate([mask[k]] * (ft // 128), axis=1)
        low = mm3(f, down_h[layer], down_l[layer]) * live
        gath[me, :, rows(k), :] = low.reshape(eb, CHUNK, ft)

    for k in range(nk):
        ids = me * r + k * CHUNK + lax.broadcasted_iota(jnp.int32, (CHUNK, 128), 0)
        for c in range(eb):
            mask[k, c * CHUNK : (c + 1) * CHUNK, :] = jnp.where(ids < tab[o_count + c], 1.0, 0.0).astype(F32)
    loads[5].wait()
    loads[0].wait()
    for i in (2, 3, 4, 1):
        loads[i].start()

    def split_down(i, _):
        hi, lo = split(down[i])
        down_h[i] = hi
        down_l[i] = lo
        return 0

    split_down(0, 0)
    pl.semaphore_wait(barrier, 2 * (nt - 1) + 1 + ne - 1)
    for k in range(nk):
        lower(k, 0)
        ag_send(k, 0)
    for k in range(nk):
        ag_send(k, 1)
    loads[2].wait()

    def split_coef(p, _):
        hi, lo = split(coef[tab[o_perm + p]])
        c2[p, :, 0:blk] = hi
        c2[p, :, blk : 2 * blk] = lo
        return 0

    lax.fori_loop(0, slots, split_coef, 0)
    for i in (3, 4, 1):
        loads[i].wait()
    lax.fori_loop(1, layers, split_down, 0)

    def split_rest(i, _):
        hi, lo = split(up[i])
        up_h[i] = hi
        up_l[i] = lo
        hi, lo = split(dense[i])
        dense_h[i] = hi
        dense_l[i] = lo
        return 0

    lax.fori_loop(0, layers, split_rest, 0)
    for k in range(early):
        pass_on(k, 0)

    def layer_step(layer, _):
        def widen(h, pair):
            first = 2 * pair * CHUNK

            def step(c, _):
                for rank in range(ranks):
                    hi, lo = split(gath[rank, c, first : first + 2 * CHUNK, cols(h)])
                    at = rank * r + first
                    x2[h, c, at : at + 2 * CHUNK, 0:wide] = hi
                    x2[h, c, at : at + 2 * CHUNK, wide : 2 * wide] = lo
                return 0

            for k in (2 * pair, 2 * pair + 1):
                ag_arrive(k, h, a * ns + other)
                for o in range(1, nt):
                    ag_arrive(k, h, trip(o) * ns + b)
            lax.fori_loop(0, eb, step, 0, unroll=4)

        unroll = 16

        def triplets(h):
            def step(i, prev):
                for u in range(unroll):
                    p = i * unroll + u
                    keep = tab[o_same + p].astype(F32)
                    w = x2[h, tab[o_src + p]]
                    both = dot(c2[p], jnp.concatenate([w, w], axis=0))
                    prev = prev * keep + (both[:, 0:wide] + both[:, wide : 2 * wide])
                    run[p] = prev
                return prev

            lax.fori_loop(0, slots // unroll, step, jnp.zeros((blk, wide), F32))

        def gather_terms(k, h):
            def collect(t, _):
                at, has = tab[o_last + t], tab[o_has + t].astype(F32)
                for o in range(nt):
                    for i in range(ns):
                        s = b if (i == 0) == (o == 0) else other
                        first = pl.multiple_of((trip(o) * ns + s) * r + k * CHUNK, CHUNK)
                        part[i, o, t, rows(k), cols(h)] = run[at, pl.ds(first, CHUNK), :] * has
                return 0

            lax.fori_loop(0, eb, collect, 0, unroll=4)
            rs_pair(k, h).start()

        def cross(k, h):
            rs_pair(k, h).wait_recv()
            for o in range(1, nt):
                part[0, o, :, rows(k), cols(h)] = part[0, o, :, rows(k), cols(h)] + recv1[o, :, rows(k), cols(h)]
                rs_cross(k, h, o).start()
            agg[:, rows(k), cols(h)] = part[0, 0, :, rows(k), cols(h)] + recv1[0, :, rows(k), cols(h)]

        def exchange(k, h):
            total = agg[:, rows(k), cols(h)]
            for o in range(1, nt):
                rs_arrive(k, h, o)
                total = total + recv2[trip(o), :, rows(k), cols(h)]
            agg[:, rows(k), cols(h)] = total
            for o in range(1, ne):
                base = lax.rem(e + o, ne) * cap
                for s in range(cap):
                    zs[base + s, rows(k), cols(h)] = agg[tab[o_zsrc + base + s], rows(k), cols(h)]
                z_copy(k, h, o).start()

        for k in range(early, nk - 1):
            pass_on(k, 0)
        for pair in range(nk // 2):
            if pair == nk // 2 - 1:
                pass_on(nk - 1, 0)
            widen(0, pair)
        triplets(0)
        for k in range(nk):
            pass_on(k, 1)
        ag_finish(0)
        for k in range(nk):
            gather_terms(k, 0)
        for k in range(2):
            cross(k, 0)
        for pair in range(nk // 2):
            widen(1, pair)
        triplets(1)
        ag_finish(1)
        for k in range(nk):
            gather_terms(k, 1)

        @pl.when(layer > 0)
        def _():
            pl.semaphore_wait(z_free, ne - 1)

        exchange(0, 0)
        cross(0, 1)
        cross(1, 1)
        exchange(1, 0)
        for k in range(2, nk):
            cross(k, 0)
            cross(k, 1)
        exchange(0, 1)
        exchange(1, 1)
        for k in range(2, nk):
            exchange(k, 0)
            exchange(k, 1)
        for k in range(nk):
            sides = []
            for h in range(2):
                for o in range(1, ne):
                    z_arrive(k, h, o)
                sides.append(
                    jnp.concatenate(
                        [agg[c, rows(k), cols(h)] + zr[2 * k + h][tab[o_zpos + c]] for c in range(eb)], axis=0
                    )
                )
            both = jnp.concatenate(sides, axis=1)
            lifted = mm3(both, up_h[layer], up_l[layer])
            f = out[:, rows(k), :].reshape(eb * CHUNK, de)
            mixed = (f + lifted) * INV_THREE
            v = mm3(mixed, dense_h[layer], dense_l[layer])
            new = (mixed + v / (1.0 + jnp.exp(-v))) * jnp.where(layer + 1 < layers, INV_TWO, 1.0)
            out[:, rows(k), :] = new.reshape(eb, CHUNK, de)

            @pl.when(layer + 1 < layers)
            def _():
                lower(k, layer + 1)
                ag_send(k, 0)
                ag_send(k, 1)
                if 2 <= k < early + 2:
                    pass_on(k - 2, 0)

        @pl.when(layer + 1 < layers)
        def _():
            for o in range(1, ne):
                pl.semaphore_signal(z_free, inc=1, device_id={"edge": lax.rem(e + o, ne)}, device_id_type=MESH)

        for k in range(nk):
            for h in range(2):
                rs_pair(k, h).wait_send()
                for o in range(1, nt):
                    rs_cross(k, h, o).wait_send()
                for o in range(1, ne):
                    z_copy(k, h, o).wait_send()
        return 0

    lax.fori_loop(0, layers, layer_step, 0)


def local(edge_feat, edge_counts, reverse, patterns, trip_count, coef, down_weight, up_weight, dense_weight):
    eb, r, de = edge_feat.shape
    nt, ns, ne = lax.axis_size("trip"), lax.axis_size("sub"), lax.axis_size("edge")
    layers, _, ft = down_weight.shape
    _, _, slots, blk, _ = coef.shape
    nk, ranks = r // CHUNK, nt * ns
    edge_rank = lax.axis_index("edge")
    cap = 2 * ((eb // 2 + ne // 2 - 1) // (ne // 2))
    i32 = jnp.int32
    ids = jnp.arange(slots, dtype=i32)
    key = jnp.where(ids < trip_count[0, 0], patterns[0, 0, :, 0], eb)
    before = (key[None, :] < key[:, None]) | ((key[None, :] == key[:, None]) & (ids[None, :] < ids[:, None]))
    rank = jnp.sum(before.astype(i32), axis=1)
    hot = (rank[None, :] == ids[:, None]).astype(i32)
    perm = jnp.sum(hot * ids[None, :], axis=1)
    source = jnp.sum(hot * patterns[0, 0, :, 1][None, :], axis=1)
    first = jnp.sum((key[None, :] < key[:, None]).astype(i32), axis=1)
    same = jnp.sum(hot * (first < rank).astype(i32)[None, :], axis=1)
    cl = jnp.arange(eb, dtype=i32)
    upto = jnp.sum((key[None, :] <= cl[:, None]).astype(i32), axis=1)
    has = jnp.any(key[None, :] == cl[:, None], axis=1).astype(i32)
    last = jnp.maximum(upto - 1, 0)
    mine = lax.dynamic_slice_in_dim(reverse, edge_rank * eb, eb)
    dev = mine // eb
    send_slot = jnp.sum(((dev[:, None] == dev[None, :]) & (cl[None, :] < cl[:, None])).astype(i32), axis=1)
    zslots = jnp.arange(ne * cap, dtype=i32)
    zsrc = jnp.sum(jnp.where(zslots[:, None] == (dev * cap + send_slot)[None, :], cl[None, :], 0), axis=1)
    all_ids = jnp.arange(reverse.shape[0], dtype=i32)
    match = (
        (all_ids[None, :] // eb == dev[:, None])
        & (all_ids[None, :] < mine[:, None])
        & (reverse[None, :] // eb == edge_rank)
    )
    zpos = dev * cap + jnp.sum(match.astype(i32), axis=1)
    tab = jnp.concatenate([perm, source, same, last, has, zsrc, zpos, edge_counts]).astype(i32)

    dims = (nt, ns, ne, eb, r, cap, slots, layers, blk, ft, de)
    vm = pltpu.VMEM
    dma = pltpu.SemaphoreType.DMA
    scratch = [vm((ne * cap, CHUNK, ft // 2), F32) for _ in range(2 * nk)] + [
        vm((slots, blk, blk), F32),
        vm(down_weight.shape, F32),
        vm(up_weight.shape, F32),
        vm(dense_weight.shape, F32),
        vm(down_weight.shape, BF16),
        vm(down_weight.shape, BF16),
        vm(up_weight.shape, BF16),
        vm(up_weight.shape, BF16),
        vm(dense_weight.shape, BF16),
        vm(dense_weight.shape, BF16),
        vm((slots, blk, 2 * blk), BF16),
        vm((2, eb, blk, ft), BF16),
        vm((slots, blk, ft // 2), F32),
        vm((ns, nt, eb, r, ft), F32),
        vm((nt, eb, r, ft), F32),
        vm((nt, eb, r, ft), F32),
        vm((eb, r, ft), F32),
        vm((ne * cap, r, ft), F32),
        vm((ranks, eb, r, ft), F32),
        vm((nk, eb * CHUNK, 128), F32),
        dma((6,)),
        dma((2 * nk, nt)),
        dma((2 * nk, nt)),
        dma((2 * nk,)),
        dma((2 * nk, nt)),
        dma((2 * nk, ranks)),
        dma((2 * nk,)),
        dma((2 * nk,)),
        dma((2 * nk, nt)),
        dma((2 * nk, nt)),
        dma((2 * nk, ne)),
        dma((2 * nk, ne)),
        pltpu.SemaphoreType.REGULAR,
    ]
    anywhere = pl.BlockSpec(memory_space=pl.ANY)
    unscaled = pl.pallas_call(
        functools.partial(kernel, dims),
        out_shape=jax.ShapeDtypeStruct(edge_feat.shape, F32),
        in_specs=[pl.BlockSpec(memory_space=pltpu.SMEM)] + [anywhere] * 5,
        out_specs=pl.BlockSpec(memory_space=pltpu.VMEM),
        scratch_shapes=scratch,
        compiler_params=pltpu.CompilerParams(collective_id=0, has_side_effects=True, vmem_limit_bytes=64 * 1024 * 1024 - 65536),
    )(tab, edge_feat, coef[0, 0], down_weight, up_weight, dense_weight)
    return unscaled * INV_TWO


def solution(mesh):
    placed = (
        P(("groups", "edge"), ("trip", "sub"), None),
        P(("groups", "edge")),
        P("groups"),
        P(("groups", "edge"), ("trip", "sub"), None, None),
        P(("groups", "edge"), ("trip", "sub")),
        P(("groups", "edge"), ("trip", "sub"), None, None, None),
        P(),
        P(),
        P(),
    )
    return jax.shard_map(
        local,
        mesh=mesh,
        in_specs=placed,
        out_specs=P(("groups", "edge"), ("trip", "sub"), None),
        check_vma=False,
    )
```

```python
import functools

import jax
import jax.numpy as jnp
from jax import lax
from jax.experimental import pallas as pl
from jax.experimental.pallas import tpu as pltpu
from jax.sharding import PartitionSpec as P

INV_THREE = 1.0 / 3.0**0.5
INV_TWO = 1.0 / 2.0**0.5
F32, BF16 = jnp.float32, jnp.bfloat16
MESH = pl.DeviceIdType.MESH
CHUNK = 8


def split(x):
    hi = x.astype(BF16)
    return hi, (x - hi.astype(F32)).astype(BF16)


def dot(a, b):
    return jnp.dot(a, b, preferred_element_type=F32)


def mm3(x, w_hi, w_lo):
    rows = x.shape[0]
    hi, lo = split(x)
    both = dot(jnp.concatenate([hi, lo], axis=0), w_hi)
    return both[:rows] + both[rows:] + dot(hi, w_lo)


def build_tables(dims, e, live_slots, pattern, rev, table):
    nt, ns, ne, eb, r, cap, slots, layers, blk, ft, de = dims

    def down_rows(cond, value):
        return jnp.sum(jnp.where(cond, value, 0), axis=0, keepdims=True)

    def along(cond, value):
        return jnp.sum(jnp.where(cond, value, 0), axis=1, keepdims=True)

    def put(row, value, size):
        table[row : row + 1, 0 : value.shape[1]] = jnp.minimum(jnp.maximum(value, 0), size - 1)

    def grids(n):
        return (lax.broadcasted_iota(jnp.int32, (n, n), d) for d in (0, 1))

    i, j = grids(slots)
    key_j = jnp.where(j < live_slots[...], pattern[0:1, :], eb)
    key, source = along(i == j, key_j), along(i == j, pattern[1:2, :])
    rank = along((key_j < key) | ((key_j == key) & (j < i)), 1)
    again = jnp.minimum(along((key_j == key) & (j < i), 1), 1)
    hot = rank == j
    put(0, down_rows(hot, i), slots)
    put(1, down_rows(hot, source), eb)
    put(2, down_rows(hot, again), 2)
    put(3, down_rows(key <= j, 1) - 1, slots)
    put(4, down_rows(key == j, 1), 2)

    i, j = grids(ne * eb)

    def owner(x):
        return sum((x >= d * eb).astype(jnp.int32) for d in range(1, ne))

    to_j = rev[...]
    to = along(i == j, to_j)
    of_i, of_j, of_to = owner(i), owner(j), owner(to)
    slot = along((j < i) & (of_j == of_i) & (owner(to_j) == of_to), 1)
    base = e * eb
    put(5, down_rows((of_i == e) & (of_to * cap + slot == j), i - base), eb)
    put(6, down_rows(to == j + base, of_i * cap + slot), ne * cap)


def kernel(dims, counts, live_slots, pattern, rev, feat_hbm, coef_hbm, down_hbm, up_hbm, dense_hbm, out, *scratch):
    nt, ns, ne, eb, r, cap, slots, layers, blk, ft, de = dims
    nk, ranks, wide = r // CHUNK, nt * ns, ft // 2
    early = nk - 2 if nk > 2 else 0
    zr, scratch = scratch[: 2 * nk], scratch[2 * nk :]
    (coef, down, up, dense, down_h, down_l, up_h, up_l, dense_h, dense_l, c2, x2, run, part, recv1, recv2, agg, zs, gath, mask, table, tab,
     tab_sem, in_sem, agx_s, agy_s, agp_s, agf_s, ag_r, r1_s, r1_r, r2_s, r2_r, z_s, z_r, z_free) = scratch
    a, b, e = lax.axis_index("trip"), lax.axis_index("sub"), lax.axis_index("edge")
    other = lax.rem(b + 1, ns)
    me = a * ns + b

    rest = pl.ds(1, layers - 1)
    loads = [
        pltpu.make_async_copy(s, d, in_sem.at[i])
        for i, (s, d) in enumerate(((feat_hbm, out), (down_hbm.at[rest], down.at[rest]), (coef_hbm, coef), (up_hbm, up), (dense_hbm, dense), (down_hbm.at[0], down.at[0])))
    ]
    loads[5].start()
    loads[0].start()

    barrier = pltpu.get_barrier_semaphore()
    for o in range(1, nt):
        for s in (b, other):
            pl.semaphore_signal(barrier, inc=1, device_id={"trip": lax.rem(a + o, nt), "sub": s}, device_id_type=MESH)
    pl.semaphore_signal(barrier, inc=1, device_id={"sub": other}, device_id_type=MESH)
    for o in range(1, ne):
        pl.semaphore_signal(barrier, inc=1, device_id={"edge": lax.rem(e + o, ne)}, device_id_type=MESH)

    def rows(k):
        return pl.ds(k * CHUNK, CHUNK)

    def cols(h):
        return pl.ds(h * wide, wide)

    def remote(src, dst, send, recv, where):
        return pltpu.make_async_remote_copy(
            src_ref=src, dst_ref=dst, send_sem=send, recv_sem=recv, device_id=where, device_id_type=MESH
        )

    def trip(o):
        return lax.rem(a + o, nt)

    def both_cores(k, h):
        return False

    def gather_piece(rank, k, h):
        return gath.at[rank, :, rows(k), cols(h)]

    def ag_far(k, h, o):
        g = gather_piece(me, k, h)
        return remote(g, g, agx_s.at[2 * k + h, o], ag_r.at[2 * k + h, me], {"trip": trip(o), "sub": other})

    def ag_near(k, h, o):
        g = gather_piece(me, k, h)
        return remote(g, g, agy_s.at[2 * k + h, o], ag_r.at[2 * k + h, me], {"trip": trip(o), "sub": b})

    def ag_pair(k, h):
        g = gather_piece(me, k, h)
        return remote(g, g, agp_s.at[2 * k + h], ag_r.at[2 * k + h, me], {"sub": other})

    def ag_forward(k, h, o):
        rank = trip(o) * ns + other
        g = gather_piece(rank, k, h)
        return remote(g, g, agf_s.at[2 * k + h, o], ag_r.at[2 * k + h, rank], {"sub": other})

    def ag_arrive(k, h, rank):
        g = gather_piece(rank, k, h)
        remote(g, g, agp_s.at[2 * k + h], ag_r.at[2 * k + h, rank], {"sub": other}).wait_recv()

    def ag_send(k, h):
        for o in range(1, nt):
            ag_far(k, h, o).start()
            if both_cores(k, h):
                ag_near(k, h, o).start()
        ag_pair(k, h).start()

    def pass_on(k, h):
        for o in range(1, nt):
            ag_arrive(k, h, trip(o) * ns + other)
            if not both_cores(k, h):
                ag_forward(k, h, o).start()

    def ag_finish(h):
        for k in range(nk):
            ag_pair(k, h).wait_send()
            for o in range(1, nt):
                ag_far(k, h, o).wait_send()
                if both_cores(k, h):
                    ag_near(k, h, o).wait_send()
                else:
                    ag_forward(k, h, o).wait_send()

    def rs_pair(k, h):
        return remote(
            part.at[1, :, :, rows(k), cols(h)],
            recv1.at[:, :, rows(k), cols(h)],
            r1_s.at[2 * k + h],
            r1_r.at[2 * k + h],
            {"sub": other},
        )

    def rs_cross(k, h, o):
        return remote(
            part.at[0, o, :, rows(k), cols(h)],
            recv2.at[a, :, rows(k), cols(h)],
            r2_s.at[2 * k + h, o],
            r2_r.at[2 * k + h, a],
            {"trip": trip(o), "sub": other},
        )

    def rs_arrive(k, h, o):
        src = trip(o)
        dst = recv2.at[src, :, rows(k), cols(h)]
        remote(dst, dst, r2_s.at[2 * k + h, o], r2_r.at[2 * k + h, src], {"trip": src, "sub": other}).wait_recv()

    def z_copy(k, h, o):
        peer = lax.rem(e + o, ne)
        return remote(
            zs.at[pl.ds(peer * cap, cap), rows(k), cols(h)],
            zr[2 * k + h].at[pl.ds(e * cap, cap)],
            z_s.at[2 * k + h, o],
            z_r.at[2 * k + h, e],
            {"edge": peer},
        )

    def z_arrive(k, h, o):
        src = lax.rem(e + o, ne)
        dst = zr[2 * k + h].at[pl.ds(src * cap, cap)]
        remote(dst, dst, z_s.at[2 * k + h, o], z_r.at[2 * k + h, src], {"edge": src}).wait_recv()

    def lower(k, layer):
        f = out[:, rows(k), :].reshape(eb * CHUNK, de)
        live = jnp.concatenate([mask[k]] * (ft // 128), axis=1)
        low = mm3(f, down_h[layer], down_l[layer]) * live
        gath[me, :, rows(k), :] = low.reshape(eb, CHUNK, ft)

    for k in range(nk):
        ids = me * r + k * CHUNK + lax.broadcasted_iota(jnp.int32, (CHUNK, 128), 0)
        for c in range(eb):
            mask[k, c * CHUNK : (c + 1) * CHUNK, :] = jnp.where(ids < counts[c], 1.0, 0.0).astype(F32)
    loads[5].wait()
    loads[0].wait()
    for i in (2, 3, 4, 1):
        loads[i].start()

    def split_down(i, _):
        hi, lo = split(down[i])
        down_h[i] = hi
        down_l[i] = lo
        return 0

    split_down(0, 0)
    pl.semaphore_wait(barrier, 2 * (nt - 1) + 1 + ne - 1)
    for k in range(nk):
        lower(k, 0)
        ag_send(k, 0)
    for k in range(nk):
        ag_send(k, 1)
    build_tables(dims, e, live_slots, pattern, rev, table)
    to_scalar = pltpu.make_async_copy(table, tab, tab_sem)
    to_scalar.start()
    loads[2].wait()

    def split_coef(p, _):
        hi, lo = split(coef[p])
        c2[p, :, 0:blk] = hi
        c2[p, :, blk : 2 * blk] = lo
        return 0

    lax.fori_loop(0, slots, split_coef, 0)
    for i in (3, 4, 1):
        loads[i].wait()
    lax.fori_loop(1, layers, split_down, 0)

    def split_rest(i, _):
        hi, lo = split(up[i])
        up_h[i] = hi
        up_l[i] = lo
        hi, lo = split(dense[i])
        dense_h[i] = hi
        dense_l[i] = lo
        return 0

    lax.fori_loop(0, layers, split_rest, 0)
    to_scalar.wait()
    for k in range(early):
        pass_on(k, 0)

    def layer_step(layer, _):
        def widen(h, pair):
            first = 2 * pair * CHUNK

            def step(c, _):
                for rank in range(ranks):
                    hi, lo = split(gath[rank, c, first : first + 2 * CHUNK, cols(h)])
                    at = rank * r + first
                    x2[h, c, at : at + 2 * CHUNK, 0:wide] = hi
                    x2[h, c, at : at + 2 * CHUNK, wide : 2 * wide] = lo
                return 0

            for k in (2 * pair, 2 * pair + 1):
                ag_arrive(k, h, a * ns + other)
                for o in range(1, nt):
                    ag_arrive(k, h, trip(o) * ns + b)
            lax.fori_loop(0, eb, step, 0, unroll=4)

        unroll = slots

        def triplets(h):
            def step(i, prev):
                for u in range(unroll):
                    p = i * unroll + u
                    keep = tab[2, p].astype(F32)
                    w = x2[h, tab[1, p]]
                    both = dot(c2[tab[0, p]], jnp.concatenate([w, w], axis=0))
                    prev = prev * keep + (both[:, 0:wide] + both[:, wide : 2 * wide])
                    run[p] = prev
                return prev

            lax.fori_loop(0, slots // unroll, step, jnp.zeros((blk, wide), F32))

        def gather_terms(k, h):
            def collect(t, _):
                at, has = tab[3, t], tab[4, t].astype(F32)
                for o in range(nt):
                    for i in range(ns):
                        s = b if (i == 0) == (o == 0) else other
                        first = pl.multiple_of((trip(o) * ns + s) * r + k * CHUNK, CHUNK)
                        part[i, o, t, rows(k), cols(h)] = run[at, pl.ds(first, CHUNK), :] * has
                return 0

            lax.fori_loop(0, eb, collect, 0, unroll=4)
            rs_pair(k, h).start()

        def cross(k, h):
            rs_pair(k, h).wait_recv()
            for o in range(1, nt):
                part[0, o, :, rows(k), cols(h)] = part[0, o, :, rows(k), cols(h)] + recv1[o, :, rows(k), cols(h)]
                rs_cross(k, h, o).start()
            agg[:, rows(k), cols(h)] = part[0, 0, :, rows(k), cols(h)] + recv1[0, :, rows(k), cols(h)]

        def exchange(k, h):
            total = agg[:, rows(k), cols(h)]
            for o in range(1, nt):
                rs_arrive(k, h, o)
                total = total + recv2[trip(o), :, rows(k), cols(h)]
            agg[:, rows(k), cols(h)] = total
            for o in range(1, ne):
                base = lax.rem(e + o, ne) * cap
                for s in range(cap):
                    zs[base + s, rows(k), cols(h)] = agg[tab[5, base + s], rows(k), cols(h)]
                z_copy(k, h, o).start()

        for k in range(early, nk - 1):
            pass_on(k, 0)
        for pair in range(nk // 2):
            if pair == nk // 2 - 1:
                pass_on(nk - 1, 0)
            widen(0, pair)
        triplets(0)
        for k in range(nk):
            pass_on(k, 1)
        ag_finish(0)
        for k in range(nk):
            gather_terms(k, 0)
        for k in range(2):
            cross(k, 0)
        for pair in range(nk // 2):
            widen(1, pair)
        triplets(1)
        ag_finish(1)
        for k in range(nk):
            gather_terms(k, 1)

        @pl.when(layer > 0)
        def _():
            pl.semaphore_wait(z_free, ne - 1)

        exchange(0, 0)
        cross(0, 1)
        cross(1, 1)
        exchange(1, 0)
        for k in range(2, nk):
            cross(k, 0)
            cross(k, 1)
        exchange(0, 1)
        exchange(1, 1)
        for k in range(2, nk):
            exchange(k, 0)
            exchange(k, 1)
        for k in range(nk):
            sides = []
            for h in range(2):
                for o in range(1, ne):
                    z_arrive(k, h, o)
                sides.append(
                    jnp.concatenate(
                        [agg[c, rows(k), cols(h)] + zr[2 * k + h][tab[6, c]] for c in range(eb)], axis=0
                    )
                )
            both = jnp.concatenate(sides, axis=1)
            lifted = mm3(both, up_h[layer], up_l[layer])
            f = out[:, rows(k), :].reshape(eb * CHUNK, de)
            mixed = (f + lifted) * INV_THREE
            v = mm3(mixed, dense_h[layer], dense_l[layer])
            new = (mixed + v / (1.0 + jnp.exp(-v))) * jnp.where(layer + 1 < layers, INV_TWO, 1.0)
            out[:, rows(k), :] = new.reshape(eb, CHUNK, de)

            @pl.when(layer + 1 < layers)
            def _():
                lower(k, layer + 1)
                ag_send(k, 0)
                ag_send(k, 1)
                if 2 <= k < early + 2:
                    pass_on(k - 2, 0)

        @pl.when(layer + 1 < layers)
        def _():
            for o in range(1, ne):
                pl.semaphore_signal(z_free, inc=1, device_id={"edge": lax.rem(e + o, ne)}, device_id_type=MESH)

        for k in range(nk):
            for h in range(2):
                rs_pair(k, h).wait_send()
                for o in range(1, nt):
                    rs_cross(k, h, o).wait_send()
                for o in range(1, ne):
                    z_copy(k, h, o).wait_send()
        return 0

    lax.fori_loop(0, layers, layer_step, 0)


def local(edge_feat, edge_counts, reverse, patterns, trip_count, coef, down_weight, up_weight, dense_weight):
    eb, r, de = edge_feat.shape
    nt, ns, ne = lax.axis_size("trip"), lax.axis_size("sub"), lax.axis_size("edge")
    layers, _, ft = down_weight.shape
    _, _, slots, blk, _ = coef.shape
    nk, ranks = r // CHUNK, nt * ns
    cap = 2 * ((eb // 2 + ne // 2 - 1) // (ne // 2))
    dims = (nt, ns, ne, eb, r, cap, slots, layers, blk, ft, de)
    vm = pltpu.VMEM
    dma = pltpu.SemaphoreType.DMA
    scratch = [vm((ne * cap, CHUNK, ft // 2), F32) for _ in range(2 * nk)] + [
        vm((slots, blk, blk), F32),
        vm(down_weight.shape, F32),
        vm(up_weight.shape, F32),
        vm(dense_weight.shape, F32),
        vm(down_weight.shape, BF16),
        vm(down_weight.shape, BF16),
        vm(up_weight.shape, BF16),
        vm(up_weight.shape, BF16),
        vm(dense_weight.shape, BF16),
        vm(dense_weight.shape, BF16),
        vm((slots, blk, 2 * blk), BF16),
        vm((2, eb, blk, ft), BF16),
        vm((slots, blk, ft // 2), F32),
        vm((ns, nt, eb, r, ft), F32),
        vm((nt, eb, r, ft), F32),
        vm((nt, eb, r, ft), F32),
        vm((eb, r, ft), F32),
        vm((ne * cap, r, ft), F32),
        vm((ranks, eb, r, ft), F32),
        vm((nk, eb * CHUNK, 128), F32),
        vm((8, max(128, ne * eb, slots)), jnp.int32),
        pltpu.SMEM((8, max(128, ne * eb, slots)), jnp.int32),
        dma,
        dma((6,)),
        dma((2 * nk, nt)),
        dma((2 * nk, nt)),
        dma((2 * nk,)),
        dma((2 * nk, nt)),
        dma((2 * nk, ranks)),
        dma((2 * nk,)),
        dma((2 * nk,)),
        dma((2 * nk, nt)),
        dma((2 * nk, nt)),
        dma((2 * nk, ne)),
        dma((2 * nk, ne)),
        pltpu.SemaphoreType.REGULAR,
    ]
    anywhere = pl.BlockSpec(memory_space=pl.ANY)
    unscaled = pl.pallas_call(
        functools.partial(kernel, dims),
        out_shape=jax.ShapeDtypeStruct(edge_feat.shape, F32),
        in_specs=[pl.BlockSpec(memory_space=pltpu.SMEM)] + [pl.BlockSpec(memory_space=pltpu.VMEM)] * 3 + [anywhere] * 5,
        out_specs=pl.BlockSpec(memory_space=pltpu.VMEM),
        scratch_shapes=scratch,
        compiler_params=pltpu.CompilerParams(collective_id=0, has_side_effects=True, vmem_limit_bytes=64 * 1024 * 1024 - 65536),
    )(edge_counts, trip_count, patterns[0, 0].T, reverse[None, :], edge_feat, coef[0, 0], down_weight, up_weight, dense_weight)
    return unscaled * INV_TWO


def solution(mesh):
    placed = (
        P(("groups", "edge"), ("trip", "sub"), None),
        P(("groups", "edge")),
        P("groups"),
        P(("groups", "edge"), ("trip", "sub"), None, None),
        P(("groups", "edge"), ("trip", "sub")),
        P(("groups", "edge"), ("trip", "sub"), None, None, None),
        P(),
        P(),
        P(),
    )
    return jax.shard_map(
        local,
        mesh=mesh,
        in_specs=placed,
        out_specs=P(("groups", "edge"), ("trip", "sub"), None),
        check_vma=False,
    )
```

```python
import functools

import jax
import jax.numpy as jnp
from jax import lax
from jax.experimental import pallas as pl
from jax.experimental.pallas import tpu as pltpu
from jax.sharding import PartitionSpec as P

INV_THREE = 1.0 / 3.0**0.5
INV_TWO = 1.0 / 2.0**0.5
F32, BF16 = jnp.float32, jnp.bfloat16
MESH = pl.DeviceIdType.MESH
CHUNK = 8


def split(x):
    hi = x.astype(BF16)
    return hi, (x - hi.astype(F32)).astype(BF16)


def dot(a, b):
    return jnp.dot(a, b, preferred_element_type=F32)


def mm3(x, w_hi, w_lo):
    rows = x.shape[0]
    hi, lo = split(x)
    both = dot(jnp.concatenate([hi, lo], axis=0), w_hi)
    return both[:rows] + both[rows:] + dot(hi, w_lo)


def build_tables(dims, e, live_slots, pattern, rev, table):
    nt, ns, ne, eb, r, cap, slots, layers, blk, ft, de = dims

    def down_rows(cond, value):
        return jnp.sum(jnp.where(cond, value, 0), axis=0, keepdims=True)

    def along(cond, value):
        return jnp.sum(jnp.where(cond, value, 0), axis=1, keepdims=True)

    def put(row, value, size):
        table[row : row + 1, 0 : value.shape[1]] = jnp.minimum(jnp.maximum(value, 0), size - 1)

    def grids(n):
        return (lax.broadcasted_iota(jnp.int32, (n, n), d) for d in (0, 1))

    i, j = grids(slots)
    key_j = jnp.where(j < live_slots[...], pattern[0:1, :], eb)
    key, source = along(i == j, key_j), along(i == j, pattern[1:2, :])
    rank = along((key_j < key) | ((key_j == key) & (j < i)), 1)
    again = jnp.minimum(along((key_j == key) & (j < i), 1), 1)
    hot = rank == j
    put(0, down_rows(hot, i), slots)
    put(1, down_rows(hot, source), eb)
    put(2, down_rows(hot, again), 2)
    put(3, down_rows(key <= j, 1) - 1, slots)
    put(4, down_rows(key == j, 1), 2)

    i, j = grids(ne * eb)

    def owner(x):
        return sum((x >= d * eb).astype(jnp.int32) for d in range(1, ne))

    to_j = rev[...]
    to = along(i == j, to_j)
    of_i, of_j, of_to = owner(i), owner(j), owner(to)
    slot = along((j < i) & (of_j == of_i) & (owner(to_j) == of_to), 1)
    base = e * eb
    put(5, down_rows((of_i == e) & (of_to * cap + slot == j), i - base), eb)
    put(6, down_rows(to == j + base, of_i * cap + slot), ne * cap)


def kernel(dims, counts, live_slots, pattern, rev, feat_hbm, coef_hbm, down_hbm, up_hbm, dense_hbm, out_hbm, *scratch):
    nt, ns, ne, eb, r, cap, slots, layers, blk, ft, de = dims
    nk, ranks, wide = r // CHUNK, nt * ns, ft // 2
    early = nk - 2 if nk > 2 else 0
    zr, scratch = scratch[: 2 * nk], scratch[2 * nk :]
    (out, coef, down, up, dense, down_h, down_l, up_h, up_l, dense_h, dense_l, c2, x2, run, part, recv1, recv2, agg, zs, gath, mask, table, tab,
     tab_sem, out_sem, in_sem, agx_s, agy_s, agp_s, agf_s, ag_r, r1_s, r1_r, r2_s, r2_r, z_s, z_r, z_free) = scratch
    a, b, e = lax.axis_index("trip"), lax.axis_index("sub"), lax.axis_index("edge")
    other = lax.rem(b + 1, ns)
    me = a * ns + b

    rest = pl.ds(1, layers - 1)
    loads = [
        pltpu.make_async_copy(s, d, in_sem.at[i])
        for i, (s, d) in enumerate([(feat_hbm.at[:, pl.ds(k * CHUNK, CHUNK), :], out.at[:, pl.ds(k * CHUNK, CHUNK), :]) for k in range(nk)] + [(down_hbm.at[rest], down.at[rest]), (coef_hbm, coef), (up_hbm, up), (dense_hbm, dense), (down_hbm.at[0], down.at[0])])
    ]
    l_down, l_coef, l_up, l_dense, l_first = range(nk, nk + 5)
    loads[l_first].start()
    for k in range(nk):
        loads[k].start()

    barrier = pltpu.get_barrier_semaphore()
    for o in range(1, nt):
        for s in (b, other):
            pl.semaphore_signal(barrier, inc=1, device_id={"trip": lax.rem(a + o, nt), "sub": s}, device_id_type=MESH)
    pl.semaphore_signal(barrier, inc=1, device_id={"sub": other}, device_id_type=MESH)
    for o in range(1, ne):
        pl.semaphore_signal(barrier, inc=1, device_id={"edge": lax.rem(e + o, ne)}, device_id_type=MESH)

    def rows(k):
        return pl.ds(k * CHUNK, CHUNK)

    def cols(h):
        return pl.ds(h * wide, wide)

    def remote(src, dst, send, recv, where):
        return pltpu.make_async_remote_copy(
            src_ref=src, dst_ref=dst, send_sem=send, recv_sem=recv, device_id=where, device_id_type=MESH
        )

    def finished(k):
        return pltpu.make_async_copy(out.at[:, rows(k), :], out_hbm.at[:, rows(k), :], out_sem.at[k])

    def trip(o):
        return lax.rem(a + o, nt)

    def both_cores(k, h):
        return False

    def gather_piece(rank, k, h):
        return gath.at[rank, :, rows(k), cols(h)]

    def ag_far(k, h, o):
        g = gather_piece(me, k, h)
        return remote(g, g, agx_s.at[2 * k + h, o], ag_r.at[2 * k + h, me], {"trip": trip(o), "sub": other})

    def ag_near(k, h, o):
        g = gather_piece(me, k, h)
        return remote(g, g, agy_s.at[2 * k + h, o], ag_r.at[2 * k + h, me], {"trip": trip(o), "sub": b})

    def ag_pair(k, h):
        g = gather_piece(me, k, h)
        return remote(g, g, agp_s.at[2 * k + h], ag_r.at[2 * k + h, me], {"sub": other})

    def ag_forward(k, h, o):
        rank = trip(o) * ns + other
        g = gather_piece(rank, k, h)
        return remote(g, g, agf_s.at[2 * k + h, o], ag_r.at[2 * k + h, rank], {"sub": other})

    def ag_arrive(k, h, rank):
        g = gather_piece(rank, k, h)
        remote(g, g, agp_s.at[2 * k + h], ag_r.at[2 * k + h, rank], {"sub": other}).wait_recv()

    def ag_send(k, h):
        for o in range(1, nt):
            ag_far(k, h, o).start()
            if both_cores(k, h):
                ag_near(k, h, o).start()
        ag_pair(k, h).start()

    def pass_on(k, h):
        for o in range(1, nt):
            ag_arrive(k, h, trip(o) * ns + other)
            if not both_cores(k, h):
                ag_forward(k, h, o).start()

    def ag_finish(h):
        for k in range(nk):
            ag_pair(k, h).wait_send()
            for o in range(1, nt):
                ag_far(k, h, o).wait_send()
                if both_cores(k, h):
                    ag_near(k, h, o).wait_send()
                else:
                    ag_forward(k, h, o).wait_send()

    def rs_pair(k, h):
        return remote(
            part.at[1, :, :, rows(k), cols(h)],
            recv1.at[:, :, rows(k), cols(h)],
            r1_s.at[2 * k + h],
            r1_r.at[2 * k + h],
            {"sub": other},
        )

    def rs_cross(k, h, o):
        return remote(
            part.at[0, o, :, rows(k), cols(h)],
            recv2.at[a, :, rows(k), cols(h)],
            r2_s.at[2 * k + h, o],
            r2_r.at[2 * k + h, a],
            {"trip": trip(o), "sub": other},
        )

    def rs_arrive(k, h, o):
        src = trip(o)
        dst = recv2.at[src, :, rows(k), cols(h)]
        remote(dst, dst, r2_s.at[2 * k + h, o], r2_r.at[2 * k + h, src], {"trip": src, "sub": other}).wait_recv()

    def z_copy(k, h, o):
        peer = lax.rem(e + o, ne)
        return remote(
            zs.at[pl.ds(peer * cap, cap), rows(k), cols(h)],
            zr[2 * k + h].at[pl.ds(e * cap, cap)],
            z_s.at[2 * k + h, o],
            z_r.at[2 * k + h, e],
            {"edge": peer},
        )

    def z_arrive(k, h, o):
        src = lax.rem(e + o, ne)
        dst = zr[2 * k + h].at[pl.ds(src * cap, cap)]
        remote(dst, dst, z_s.at[2 * k + h, o], z_r.at[2 * k + h, src], {"edge": src}).wait_recv()

    def lower(k, layer):
        f = out[:, rows(k), :].reshape(eb * CHUNK, de)
        live = jnp.concatenate([mask[k]] * (ft // 128), axis=1)
        low = mm3(f, down_h[layer], down_l[layer]) * live
        gath[me, :, rows(k), :] = low.reshape(eb, CHUNK, ft)

    for k in range(nk):
        ids = me * r + k * CHUNK + lax.broadcasted_iota(jnp.int32, (CHUNK, 128), 0)
        for c in range(eb):
            mask[k, c * CHUNK : (c + 1) * CHUNK, :] = jnp.where(ids < counts[c], 1.0, 0.0).astype(F32)
    loads[l_first].wait()
    for i in (l_coef, l_up, l_dense, l_down):
        loads[i].start()

    def split_down(i, _):
        hi, lo = split(down[i])
        down_h[i] = hi
        down_l[i] = lo
        return 0

    split_down(0, 0)
    for k in range(nk):
        loads[k].wait()
        lower(k, 0)
        if k == 0:
            pl.semaphore_wait(barrier, 2 * (nt - 1) + 1 + ne - 1)
        ag_send(k, 0)
    for k in range(nk):
        ag_send(k, 1)
    build_tables(dims, e, live_slots, pattern, rev, table)
    to_scalar = pltpu.make_async_copy(table, tab, tab_sem)
    to_scalar.start()
    loads[l_coef].wait()

    def split_coef(p, _):
        hi, lo = split(coef[p])
        c2[p, :, 0:blk] = hi
        c2[p, :, blk : 2 * blk] = lo
        return 0

    lax.fori_loop(0, slots, split_coef, 0)
    for i in (l_up, l_dense, l_down):
        loads[i].wait()
    lax.fori_loop(1, layers, split_down, 0)

    def split_rest(i, _):
        hi, lo = split(up[i])
        up_h[i] = hi
        up_l[i] = lo
        hi, lo = split(dense[i])
        dense_h[i] = hi
        dense_l[i] = lo
        return 0

    lax.fori_loop(0, layers, split_rest, 0)
    to_scalar.wait()
    for k in range(early):
        pass_on(k, 0)

    def layer_step(layer, _):
        def widen(h, pair):
            first = 2 * pair * CHUNK

            def step(c, _):
                for rank in range(ranks):
                    hi, lo = split(gath[rank, c, first : first + 2 * CHUNK, cols(h)])
                    at = rank * r + first
                    x2[h, c, at : at + 2 * CHUNK, 0:wide] = hi
                    x2[h, c, at : at + 2 * CHUNK, wide : 2 * wide] = lo
                return 0

            for k in (2 * pair, 2 * pair + 1):
                ag_arrive(k, h, a * ns + other)
                for o in range(1, nt):
                    ag_arrive(k, h, trip(o) * ns + b)
            lax.fori_loop(0, eb, step, 0, unroll=eb)

        unroll = slots

        def triplets(h):
            def step(i, prev):
                for u in range(unroll):
                    p = i * unroll + u
                    keep = tab[2, p].astype(F32)
                    w = x2[h, tab[1, p]]
                    both = dot(c2[tab[0, p]], jnp.concatenate([w, w], axis=0))
                    prev = prev * keep + (both[:, 0:wide] + both[:, wide : 2 * wide])
                    run[p] = prev
                return prev

            lax.fori_loop(0, slots // unroll, step, jnp.zeros((blk, wide), F32))

        def gather_terms(k, h):
            def collect(t, _):
                at, has = tab[3, t], tab[4, t].astype(F32)
                for o in range(nt):
                    for i in range(ns):
                        s = b if (i == 0) == (o == 0) else other
                        first = pl.multiple_of((trip(o) * ns + s) * r + k * CHUNK, CHUNK)
                        part[i, o, t, rows(k), cols(h)] = run[at, pl.ds(first, CHUNK), :] * has
                return 0

            lax.fori_loop(0, eb, collect, 0, unroll=eb)
            rs_pair(k, h).start()

        def cross(k, h):
            rs_pair(k, h).wait_recv()
            for o in range(1, nt):
                part[0, o, :, rows(k), cols(h)] = part[0, o, :, rows(k), cols(h)] + recv1[o, :, rows(k), cols(h)]
                rs_cross(k, h, o).start()
            agg[:, rows(k), cols(h)] = part[0, 0, :, rows(k), cols(h)] + recv1[0, :, rows(k), cols(h)]

        def exchange(k, h):
            total = agg[:, rows(k), cols(h)]
            for o in range(1, nt):
                rs_arrive(k, h, o)
                total = total + recv2[trip(o), :, rows(k), cols(h)]
            agg[:, rows(k), cols(h)] = total
            for o in range(1, ne):
                base = lax.rem(e + o, ne) * cap
                for s in range(cap):
                    zs[base + s, rows(k), cols(h)] = agg[tab[5, base + s], rows(k), cols(h)]
                z_copy(k, h, o).start()

        for k in range(early, nk - 1):
            pass_on(k, 0)
        for pair in range(nk // 2):
            if pair == nk // 2 - 1:
                pass_on(nk - 1, 0)
            widen(0, pair)
        triplets(0)
        gather_terms(0, 0)
        gather_terms(1, 0)
        for k in range(nk):
            pass_on(k, 1)
        cross(0, 0)
        cross(1, 0)
        for k in range(2, nk):
            gather_terms(k, 0)
        for pair in range(nk // 2):
            widen(1, pair)
        triplets(1)

        @pl.when(layer > 0)
        def _():
            pl.semaphore_wait(z_free, ne - 1)

        exchange(0, 0)
        ag_finish(0)
        ag_finish(1)
        gather_terms(0, 1)
        gather_terms(1, 1)
        exchange(1, 0)
        for k in range(2, nk):
            gather_terms(k, 1)
        cross(0, 1)
        cross(1, 1)
        for k in range(2, nk):
            cross(k, 0)
            cross(k, 1)
        exchange(0, 1)
        exchange(1, 1)
        for k in range(2, nk):
            exchange(k, 0)
            exchange(k, 1)
        for k in range(nk):
            sides = []
            for h in range(2):
                for o in range(1, ne):
                    z_arrive(k, h, o)
                sides.append(
                    jnp.concatenate(
                        [agg[c, rows(k), cols(h)] + zr[2 * k + h][tab[6, c]] for c in range(eb)], axis=0
                    )
                )
            both = jnp.concatenate(sides, axis=1)
            lifted = mm3(both, up_h[layer], up_l[layer])
            f = out[:, rows(k), :].reshape(eb * CHUNK, de)
            mixed = (f + lifted) * INV_THREE
            v = mm3(mixed, dense_h[layer], dense_l[layer])
            new = (mixed + v / (1.0 + jnp.exp(-v))) * jnp.where(layer + 1 < layers, INV_TWO, 1.0)
            out[:, rows(k), :] = new.reshape(eb, CHUNK, de)

            @pl.when(layer + 1 == layers)
            def _():
                finished(k).start()

            @pl.when(layer + 1 < layers)
            def _():
                lower(k, layer + 1)
                ag_send(k, 0)
                ag_send(k, 1)
                if 2 <= k < early + 2:
                    pass_on(k - 2, 0)

        @pl.when(layer + 1 < layers)
        def _():
            for o in range(1, ne):
                pl.semaphore_signal(z_free, inc=1, device_id={"edge": lax.rem(e + o, ne)}, device_id_type=MESH)

        for k in range(nk):
            for h in range(2):
                rs_pair(k, h).wait_send()
                for o in range(1, nt):
                    rs_cross(k, h, o).wait_send()
                for o in range(1, ne):
                    z_copy(k, h, o).wait_send()
        return 0

    lax.fori_loop(0, layers, layer_step, 0)
    for k in range(nk):
        finished(k).wait()


def local(edge_feat, edge_counts, reverse, patterns, trip_count, coef, down_weight, up_weight, dense_weight):
    eb, r, de = edge_feat.shape
    nt, ns, ne = lax.axis_size("trip"), lax.axis_size("sub"), lax.axis_size("edge")
    layers, _, ft = down_weight.shape
    _, _, slots, blk, _ = coef.shape
    nk, ranks = r // CHUNK, nt * ns
    cap = 2 * ((eb // 2 + ne // 2 - 1) // (ne // 2))
    dims = (nt, ns, ne, eb, r, cap, slots, layers, blk, ft, de)
    vm = pltpu.VMEM
    dma = pltpu.SemaphoreType.DMA
    scratch = [vm((ne * cap, CHUNK, ft // 2), F32) for _ in range(2 * nk)] + [
        vm(edge_feat.shape, F32),
        vm((slots, blk, blk), F32),
        vm(down_weight.shape, F32),
        vm(up_weight.shape, F32),
        vm(dense_weight.shape, F32),
        vm(down_weight.shape, BF16),
        vm(down_weight.shape, BF16),
        vm(up_weight.shape, BF16),
        vm(up_weight.shape, BF16),
        vm(dense_weight.shape, BF16),
        vm(dense_weight.shape, BF16),
        vm((slots, blk, 2 * blk), BF16),
        vm((2, eb, blk, ft), BF16),
        vm((slots, blk, ft // 2), F32),
        vm((ns, nt, eb, r, ft), F32),
        vm((nt, eb, r, ft), F32),
        vm((nt, eb, r, ft), F32),
        vm((eb, r, ft), F32),
        vm((ne * cap, r, ft), F32),
        vm((ranks, eb, r, ft), F32),
        vm((nk, eb * CHUNK, 128), F32),
        vm((8, max(128, ne * eb, slots)), jnp.int32),
        pltpu.SMEM((8, max(128, ne * eb, slots)), jnp.int32),
        dma,
        dma((nk,)),
        dma((nk + 5,)),
        dma((2 * nk, nt)),
        dma((2 * nk, nt)),
        dma((2 * nk,)),
        dma((2 * nk, nt)),
        dma((2 * nk, ranks)),
        dma((2 * nk,)),
        dma((2 * nk,)),
        dma((2 * nk, nt)),
        dma((2 * nk, nt)),
        dma((2 * nk, ne)),
        dma((2 * nk, ne)),
        pltpu.SemaphoreType.REGULAR,
    ]
    anywhere = pl.BlockSpec(memory_space=pl.ANY)
    unscaled = pl.pallas_call(
        functools.partial(kernel, dims),
        out_shape=jax.ShapeDtypeStruct(edge_feat.shape, F32),
        in_specs=[pl.BlockSpec(memory_space=pltpu.SMEM)] + [pl.BlockSpec(memory_space=pltpu.VMEM)] * 3 + [anywhere] * 5,
        out_specs=anywhere,
        scratch_shapes=scratch,
        compiler_params=pltpu.CompilerParams(collective_id=0, has_side_effects=True, vmem_limit_bytes=64 * 1024 * 1024 - 65536),
    )(edge_counts, trip_count, patterns[0, 0].T, reverse[None, :], edge_feat, coef[0, 0], down_weight, up_weight, dense_weight)
    return unscaled * INV_TWO


def solution(mesh):
    placed = (
        P(("groups", "edge"), ("trip", "sub"), None),
        P(("groups", "edge")),
        P("groups"),
        P(("groups", "edge"), ("trip", "sub"), None, None),
        P(("groups", "edge"), ("trip", "sub")),
        P(("groups", "edge"), ("trip", "sub"), None, None, None),
        P(),
        P(),
        P(),
    )
    return jax.shard_map(
        local,
        mesh=mesh,
        in_specs=placed,
        out_specs=P(("groups", "edge"), ("trip", "sub"), None),
        check_vma=False,
    )
```

```python
import functools

import jax
import jax.numpy as jnp
from jax import lax
from jax.experimental import pallas as pl
from jax.experimental.pallas import tpu as pltpu
from jax.sharding import PartitionSpec as P

INV_THREE = 1.0 / 3.0**0.5
INV_TWO = 1.0 / 2.0**0.5
F32, BF16 = jnp.float32, jnp.bfloat16
MESH = pl.DeviceIdType.MESH
CHUNK = 8


def split(x):
    hi = x.astype(BF16)
    return hi, (x - hi.astype(F32)).astype(BF16)


def dot(a, b):
    return jnp.dot(a, b, preferred_element_type=F32)


def mm3(x, w_hi, w_lo):
    rows = x.shape[0]
    hi, lo = split(x)
    both = dot(jnp.concatenate([hi, lo], axis=0), w_hi)
    return both[:rows] + both[rows:] + dot(hi, w_lo)


def build_tables(dims, e, live_slots, pattern, rev, table):
    nt, ns, ne, eb, r, cap, slots, layers, blk, ft, de = dims

    def down_rows(cond, value):
        return jnp.sum(jnp.where(cond, value, 0), axis=0, keepdims=True)

    def along(cond, value):
        return jnp.sum(jnp.where(cond, value, 0), axis=1, keepdims=True)

    def put(row, value, size):
        table[row : row + 1, 0 : value.shape[1]] = jnp.minimum(jnp.maximum(value, 0), size - 1)

    def grids(n):
        return (lax.broadcasted_iota(jnp.int32, (n, n), d) for d in (0, 1))

    i, j = grids(slots)
    key_j = jnp.where(j < live_slots[...], pattern[0:1, :], eb)
    key, source = along(i == j, key_j), along(i == j, pattern[1:2, :])
    rank = along((key_j < key) | ((key_j == key) & (j < i)), 1)
    again = jnp.minimum(along((key_j == key) & (j < i), 1), 1)
    hot = rank == j
    put(0, down_rows(hot, i), slots)
    put(1, down_rows(hot, source), eb)
    put(2, down_rows(hot, again), 2)
    put(3, down_rows(key <= j, 1) - 1, slots)
    put(4, down_rows(key == j, 1), 2)

    i, j = grids(ne * eb)

    def owner(x):
        return sum((x >= d * eb).astype(jnp.int32) for d in range(1, ne))

    to_j = rev[...]
    to = along(i == j, to_j)
    of_i, of_j, of_to = owner(i), owner(j), owner(to)
    slot = along((j < i) & (of_j == of_i) & (owner(to_j) == of_to), 1)
    base = e * eb
    put(5, down_rows((of_i == e) & (of_to * cap + slot == j), i - base), eb)
    put(6, down_rows(to == j + base, of_i * cap + slot), ne * cap)


def kernel(dims, counts, live_slots, pattern, rev, feat_hbm, coef_hbm, down_hbm, up_hbm, dense_hbm, out_hbm, *scratch):
    nt, ns, ne, eb, r, cap, slots, layers, blk, ft, de = dims
    nk, ranks, wide = r // CHUNK, nt * ns, ft // 2
    early = nk - 2 if nk > 2 else 0
    zr, scratch = scratch[: 2 * nk], scratch[2 * nk :]
    (out, coef, down, up, dense, down_h, down_l, up_h, up_l, dense_h, dense_l, c2, x2, run, part, recv1, recv2, agg, zs, gath, mask, table, tab,
     tab_sem, out_sem, in_sem, agx_s, agp_s, agf_s, ag_r, r1_s, r1_r, r2_s, r2_r, z_s, z_r, z_free) = scratch
    a, b, e = lax.axis_index("trip"), lax.axis_index("sub"), lax.axis_index("edge")
    other = lax.rem(b + 1, ns)
    me = a * ns + b

    rest = pl.ds(1, layers - 1)
    loads = [
        pltpu.make_async_copy(s, d, in_sem.at[i])
        for i, (s, d) in enumerate([(feat_hbm.at[:, pl.ds(k * CHUNK, CHUNK), :], out.at[:, pl.ds(k * CHUNK, CHUNK), :]) for k in range(nk)] + [(down_hbm.at[rest], down.at[rest]), (coef_hbm, coef), (up_hbm, up), (dense_hbm, dense), (down_hbm.at[0], down.at[0])])
    ]
    l_down, l_coef, l_up, l_dense, l_first = range(nk, nk + 5)
    loads[l_first].start()
    for k in range(nk):
        loads[k].start()

    barrier = pltpu.get_barrier_semaphore()
    for o in range(1, nt):
        pl.semaphore_signal(barrier, inc=1, device_id={"trip": lax.rem(a + o, nt)}, device_id_type=MESH)
    pl.semaphore_signal(barrier, inc=1, device_id={"sub": other}, device_id_type=MESH)
    for o in range(1, ne):
        pl.semaphore_signal(barrier, inc=1, device_id={"edge": lax.rem(e + o, ne)}, device_id_type=MESH)

    def rows(k):
        return pl.ds(k * CHUNK, CHUNK)

    def cols(h):
        return pl.ds(h * wide, wide)

    def remote(src, dst, send, recv, where):
        return pltpu.make_async_remote_copy(
            src_ref=src, dst_ref=dst, send_sem=send, recv_sem=recv, device_id=where, device_id_type=MESH
        )

    def finished(k):
        return pltpu.make_async_copy(out.at[:, rows(k), :], out_hbm.at[:, rows(k), :], out_sem.at[k])

    def trip(o):
        return lax.rem(a + o, nt)

    def gather_piece(rank, k, h):
        return gath.at[rank, :, rows(k), cols(h)]

    def ag_far(k, h, o):
        g = gather_piece(me, k, h)
        return remote(g, g, agx_s.at[2 * k + h, o], ag_r.at[2 * k + h, me], {"trip": trip(o)})

    def ag_pair(k, h):
        g = gather_piece(me, k, h)
        return remote(g, g, agp_s.at[2 * k + h], ag_r.at[2 * k + h, me], {"sub": other})

    def ag_forward(k, h, o):
        rank = trip(o) * ns + b
        g = gather_piece(rank, k, h)
        return remote(g, g, agf_s.at[2 * k + h, o], ag_r.at[2 * k + h, rank], {"sub": other})

    def ag_arrive(k, h, rank):
        g = gather_piece(rank, k, h)
        remote(g, g, agp_s.at[2 * k + h], ag_r.at[2 * k + h, rank], {"sub": other}).wait_recv()

    def ag_send(k, h):
        for o in range(1, nt):
            ag_far(k, h, o).start()
        ag_pair(k, h).start()

    def pass_on(k, h):
        for o in range(1, nt):
            ag_arrive(k, h, trip(o) * ns + b)
            ag_forward(k, h, o).start()

    def ag_finish(h):
        for k in range(nk):
            ag_pair(k, h).wait_send()
            for o in range(1, nt):
                ag_far(k, h, o).wait_send()
                ag_forward(k, h, o).wait_send()

    def rs_pair(k, h):
        return remote(
            part.at[1, :, :, rows(k), cols(h)],
            recv1.at[:, :, rows(k), cols(h)],
            r1_s.at[2 * k + h],
            r1_r.at[2 * k + h],
            {"sub": other},
        )

    def rs_cross(k, h, o):
        return remote(
            part.at[0, o, :, rows(k), cols(h)],
            recv2.at[a, :, rows(k), cols(h)],
            r2_s.at[2 * k + h, o],
            r2_r.at[2 * k + h, a],
            {"trip": trip(o)},
        )

    def rs_arrive(k, h, o):
        src = trip(o)
        dst = recv2.at[src, :, rows(k), cols(h)]
        remote(dst, dst, r2_s.at[2 * k + h, o], r2_r.at[2 * k + h, src], {"trip": src}).wait_recv()

    def z_copy(k, h, o):
        peer = lax.rem(e + o, ne)
        return remote(
            zs.at[pl.ds(peer * cap, cap), rows(k), cols(h)],
            zr[2 * k + h].at[pl.ds(e * cap, cap)],
            z_s.at[2 * k + h, o],
            z_r.at[2 * k + h, e],
            {"edge": peer},
        )

    def z_arrive(k, h, o):
        src = lax.rem(e + o, ne)
        dst = zr[2 * k + h].at[pl.ds(src * cap, cap)]
        remote(dst, dst, z_s.at[2 * k + h, o], z_r.at[2 * k + h, src], {"edge": src}).wait_recv()

    def lower(k, layer):
        f = out[:, rows(k), :].reshape(eb * CHUNK, de)
        live = jnp.concatenate([mask[k]] * (ft // 128), axis=1)
        low = mm3(f, down_h[layer], down_l[layer]) * live
        gath[me, :, rows(k), :] = low.reshape(eb, CHUNK, ft)

    for k in range(nk):
        ids = me * r + k * CHUNK + lax.broadcasted_iota(jnp.int32, (CHUNK, 128), 0)
        for c in range(eb):
            mask[k, c * CHUNK : (c + 1) * CHUNK, :] = jnp.where(ids < counts[c], 1.0, 0.0).astype(F32)
    loads[l_first].wait()
    for i in (l_coef, l_up, l_dense, l_down):
        loads[i].start()

    def split_down(i, _):
        hi, lo = split(down[i])
        down_h[i] = hi
        down_l[i] = lo
        return 0

    split_down(0, 0)
    for k in range(nk):
        loads[k].wait()
        lower(k, 0)
        if k == 0:
            pl.semaphore_wait(barrier, nt - 1 + 1 + ne - 1)
        ag_send(k, 0)
    for k in range(nk):
        ag_send(k, 1)
    build_tables(dims, e, live_slots, pattern, rev, table)
    to_scalar = pltpu.make_async_copy(table, tab, tab_sem)
    to_scalar.start()
    loads[l_coef].wait()

    def split_coef(p, _):
        hi, lo = split(coef[p])
        c2[p, :, 0:blk] = hi
        c2[p, :, blk : 2 * blk] = lo
        return 0

    lax.fori_loop(0, slots, split_coef, 0)
    for i in (l_up, l_dense, l_down):
        loads[i].wait()
    lax.fori_loop(1, layers, split_down, 0)

    def split_rest(i, _):
        hi, lo = split(up[i])
        up_h[i] = hi
        up_l[i] = lo
        hi, lo = split(dense[i])
        dense_h[i] = hi
        dense_l[i] = lo
        return 0

    lax.fori_loop(0, layers, split_rest, 0)
    to_scalar.wait()
    for k in range(early):
        pass_on(k, 0)

    def layer_step(layer, _):
        def widen(h, pair):
            first = 2 * pair * CHUNK

            def step(c, _):
                for rank in range(ranks):
                    hi, lo = split(gath[rank, c, first : first + 2 * CHUNK, cols(h)])
                    at = rank * r + first
                    x2[h, c, at : at + 2 * CHUNK, 0:wide] = hi
                    x2[h, c, at : at + 2 * CHUNK, wide : 2 * wide] = lo
                return 0

            for k in (2 * pair, 2 * pair + 1):
                ag_arrive(k, h, a * ns + other)
                for o in range(1, nt):
                    ag_arrive(k, h, trip(o) * ns + other)
            lax.fori_loop(0, eb, step, 0, unroll=eb)

        unroll = slots

        def triplets(h):
            def step(i, prev):
                for u in range(unroll):
                    p = i * unroll + u
                    keep = tab[2, p].astype(F32)
                    w = x2[h, tab[1, p]]
                    both = dot(c2[tab[0, p]], jnp.concatenate([w, w], axis=0))
                    prev = prev * keep + (both[:, 0:wide] + both[:, wide : 2 * wide])
                    run[p] = prev
                return prev

            lax.fori_loop(0, slots // unroll, step, jnp.zeros((blk, wide), F32))

        def gather_terms(k, h):
            def collect(t, _):
                at, has = tab[3, t], tab[4, t].astype(F32)
                for o in range(nt):
                    for i in range(ns):
                        s = b if i == 0 else other
                        first = pl.multiple_of((trip(o) * ns + s) * r + k * CHUNK, CHUNK)
                        part[i, o, t, rows(k), cols(h)] = run[at, pl.ds(first, CHUNK), :] * has
                return 0

            lax.fori_loop(0, eb, collect, 0, unroll=eb)
            rs_pair(k, h).start()

        def cross(k, h):
            rs_pair(k, h).wait_recv()
            for o in range(1, nt):
                part[0, o, :, rows(k), cols(h)] = part[0, o, :, rows(k), cols(h)] + recv1[o, :, rows(k), cols(h)]
                rs_cross(k, h, o).start()
            agg[:, rows(k), cols(h)] = part[0, 0, :, rows(k), cols(h)] + recv1[0, :, rows(k), cols(h)]

        def exchange(k, h):
            total = agg[:, rows(k), cols(h)]
            for o in range(1, nt):
                rs_arrive(k, h, o)
                total = total + recv2[trip(o), :, rows(k), cols(h)]
            agg[:, rows(k), cols(h)] = total
            for o in range(1, ne):
                base = lax.rem(e + o, ne) * cap
                for s in range(cap):
                    zs[base + s, rows(k), cols(h)] = agg[tab[5, base + s], rows(k), cols(h)]
                z_copy(k, h, o).start()

        for k in range(early, nk - 1):
            pass_on(k, 0)
        for pair in range(nk // 2):
            if pair == nk // 2 - 1:
                pass_on(nk - 1, 0)
            widen(0, pair)
        triplets(0)
        gather_terms(0, 0)
        gather_terms(1, 0)
        for k in range(nk):
            pass_on(k, 1)
        cross(0, 0)
        cross(1, 0)
        for k in range(2, nk):
            gather_terms(k, 0)
        for pair in range(nk // 2):
            widen(1, pair)
        triplets(1)

        @pl.when(layer > 0)
        def _():
            pl.semaphore_wait(z_free, ne - 1)

        exchange(0, 0)
        ag_finish(0)
        ag_finish(1)
        gather_terms(0, 1)
        gather_terms(1, 1)
        exchange(1, 0)
        for k in range(2, nk):
            gather_terms(k, 1)
        cross(0, 1)
        cross(1, 1)
        for k in range(2, nk):
            cross(k, 0)
            cross(k, 1)
        exchange(0, 1)
        exchange(1, 1)
        for k in range(2, nk):
            exchange(k, 0)
            exchange(k, 1)
        for k in range(nk):
            sides = []
            for h in range(2):
                for o in range(1, ne):
                    z_arrive(k, h, o)
                sides.append(
                    jnp.concatenate(
                        [agg[c, rows(k), cols(h)] + zr[2 * k + h][tab[6, c]] for c in range(eb)], axis=0
                    )
                )
            both = jnp.concatenate(sides, axis=1)
            lifted = mm3(both, up_h[layer], up_l[layer])
            f = out[:, rows(k), :].reshape(eb * CHUNK, de)
            mixed = (f + lifted) * INV_THREE
            v = mm3(mixed, dense_h[layer], dense_l[layer])
            new = (mixed + v / (1.0 + jnp.exp(-v))) * jnp.where(layer + 1 < layers, INV_TWO, 1.0)
            out[:, rows(k), :] = new.reshape(eb, CHUNK, de)

            @pl.when(layer + 1 == layers)
            def _():
                finished(k).start()

            @pl.when(layer + 1 < layers)
            def _():
                lower(k, layer + 1)
                ag_send(k, 0)
                ag_send(k, 1)
                if 2 <= k < early + 2:
                    pass_on(k - 2, 0)

        @pl.when(layer + 1 < layers)
        def _():
            for o in range(1, ne):
                pl.semaphore_signal(z_free, inc=1, device_id={"edge": lax.rem(e + o, ne)}, device_id_type=MESH)

        for k in range(nk):
            for h in range(2):
                rs_pair(k, h).wait_send()
                for o in range(1, nt):
                    rs_cross(k, h, o).wait_send()
                for o in range(1, ne):
                    z_copy(k, h, o).wait_send()
        return 0

    lax.fori_loop(0, layers, layer_step, 0)
    for k in range(nk):
        finished(k).wait()


def local(edge_feat, edge_counts, reverse, patterns, trip_count, coef, down_weight, up_weight, dense_weight):
    eb, r, de = edge_feat.shape
    nt, ns, ne = lax.axis_size("trip"), lax.axis_size("sub"), lax.axis_size("edge")
    layers, _, ft = down_weight.shape
    _, _, slots, blk, _ = coef.shape
    nk, ranks = r // CHUNK, nt * ns
    cap = 2 * ((eb // 2 + ne // 2 - 1) // (ne // 2))
    dims = (nt, ns, ne, eb, r, cap, slots, layers, blk, ft, de)
    vm = pltpu.VMEM
    dma = pltpu.SemaphoreType.DMA
    scratch = [vm((ne * cap, CHUNK, ft // 2), F32) for _ in range(2 * nk)] + [
        vm(edge_feat.shape, F32),
        vm((slots, blk, blk), F32),
        vm(down_weight.shape, F32),
        vm(up_weight.shape, F32),
        vm(dense_weight.shape, F32),
        vm(down_weight.shape, BF16),
        vm(down_weight.shape, BF16),
        vm(up_weight.shape, BF16),
        vm(up_weight.shape, BF16),
        vm(dense_weight.shape, BF16),
        vm(dense_weight.shape, BF16),
        vm((slots, blk, 2 * blk), BF16),
        vm((2, eb, blk, ft), BF16),
        vm((slots, blk, ft // 2), F32),
        vm((ns, nt, eb, r, ft), F32),
        vm((nt, eb, r, ft), F32),
        vm((nt, eb, r, ft), F32),
        vm((eb, r, ft), F32),
        vm((ne * cap, r, ft), F32),
        vm((ranks, eb, r, ft), F32),
        vm((nk, eb * CHUNK, 128), F32),
        vm((8, max(128, ne * eb, slots)), jnp.int32),
        pltpu.SMEM((8, max(128, ne * eb, slots)), jnp.int32),
        dma,
        dma((nk,)),
        dma((nk + 5,)),
        dma((2 * nk, nt)),
        dma((2 * nk,)),
        dma((2 * nk, nt)),
        dma((2 * nk, ranks)),
        dma((2 * nk,)),
        dma((2 * nk,)),
        dma((2 * nk, nt)),
        dma((2 * nk, nt)),
        dma((2 * nk, ne)),
        dma((2 * nk, ne)),
        pltpu.SemaphoreType.REGULAR,
    ]
    anywhere = pl.BlockSpec(memory_space=pl.ANY)
    unscaled = pl.pallas_call(
        functools.partial(kernel, dims),
        out_shape=jax.ShapeDtypeStruct(edge_feat.shape, F32),
        in_specs=[pl.BlockSpec(memory_space=pltpu.SMEM)] + [pl.BlockSpec(memory_space=pltpu.VMEM)] * 3 + [anywhere] * 5,
        out_specs=anywhere,
        scratch_shapes=scratch,
        compiler_params=pltpu.CompilerParams(collective_id=0, has_side_effects=True, vmem_limit_bytes=64 * 1024 * 1024 - 65536),
    )(edge_counts, trip_count, patterns[0, 0].T, reverse[None, :], edge_feat, coef[0, 0], down_weight, up_weight, dense_weight)
    return unscaled * INV_TWO


def solution(mesh):
    placed = (
        P(("groups", "edge"), ("trip", "sub"), None),
        P(("groups", "edge")),
        P("groups"),
        P(("groups", "edge"), ("trip", "sub"), None, None),
        P(("groups", "edge"), ("trip", "sub")),
        P(("groups", "edge"), ("trip", "sub"), None, None, None),
        P(),
        P(),
        P(),
    )
    return jax.shard_map(
        local,
        mesh=mesh,
        in_specs=placed,
        out_specs=P(("groups", "edge"), ("trip", "sub"), None),
        check_vma=False,
    )
```

```python
import functools

import jax
import jax.numpy as jnp
from jax import lax
from jax.experimental import pallas as pl
from jax.experimental.pallas import tpu as pltpu
from jax.sharding import PartitionSpec as P

INV_THREE = 1.0 / 3.0**0.5
INV_TWO = 1.0 / 2.0**0.5
F32, BF16 = jnp.float32, jnp.bfloat16
MESH = pl.DeviceIdType.MESH
CHUNK = 8


def split(x):
    hi = x.astype(BF16)
    return hi, (x - hi.astype(F32)).astype(BF16)


def dot(a, b):
    return jnp.dot(a, b, preferred_element_type=F32)


def mm3(x, w_hi, w_lo):
    rows = x.shape[0]
    hi, lo = split(x)
    both = dot(jnp.concatenate([hi, lo], axis=0), w_hi)
    return both[:rows] + both[rows:] + dot(hi, w_lo)


def build_tables(dims, e, live_slots, pattern, rev, table):
    nt, ns, ne, eb, r, cap, slots, layers, blk, ft, de = dims

    def down_rows(cond, value):
        return jnp.sum(jnp.where(cond, value, 0), axis=0, keepdims=True)

    def along(cond, value):
        return jnp.sum(jnp.where(cond, value, 0), axis=1, keepdims=True)

    def put(row, value, size):
        table[row : row + 1, 0 : value.shape[1]] = jnp.minimum(jnp.maximum(value, 0), size - 1)

    def grids(n):
        return (lax.broadcasted_iota(jnp.int32, (n, n), d) for d in (0, 1))

    i, j = grids(slots)
    key_j = jnp.where(j < live_slots[...], pattern[0:1, :], eb)
    key, source = along(i == j, key_j), along(i == j, pattern[1:2, :])
    rank = along((key_j < key) | ((key_j == key) & (j < i)), 1)
    again = jnp.minimum(along((key_j == key) & (j < i), 1), 1)
    hot = rank == j
    put(0, down_rows(hot, i), slots)
    put(1, down_rows(hot, source), eb)
    put(2, down_rows(hot, again), 2)
    put(3, down_rows(key <= j, 1) - 1, slots)
    put(4, down_rows(key == j, 1), 2)

    i, j = grids(ne * eb)

    def owner(x):
        return sum((x >= d * eb).astype(jnp.int32) for d in range(1, ne))

    to_j = rev[...]
    to = along(i == j, to_j)
    of_i, of_j, of_to = owner(i), owner(j), owner(to)
    slot = along((j < i) & (of_j == of_i) & (owner(to_j) == of_to), 1)
    base = e * eb
    put(5, down_rows((of_i == e) & (of_to * cap + slot == j), i - base), eb)
    put(6, down_rows(to == j + base, of_i * cap + slot), ne * cap)


def kernel(dims, counts, live_slots, pattern, rev, feat_hbm, coef_hbm, down_hbm, up_hbm, dense_hbm, out_hbm, *scratch):
    nt, ns, ne, eb, r, cap, slots, layers, blk, ft, de = dims
    nk, ranks, wide = r // CHUNK, nt * ns, ft // 2
    early = nk - 2 if nk > 2 else 0
    zr, scratch = scratch[: 2 * nk], scratch[2 * nk :]
    (out, coef, down, up, dense, down_h, down_l, up_h, up_l, dense_h, dense_l, c2, x2, run, part, recv1, recv2, agg, zs, gath, mask, table, tab,
     tab_sem, out_sem, in_sem, agx_s, agp_s, agf_s, ag_r, r1_s, r1_r, r2_s, r2_r, z_s, z_r, z_free) = scratch
    a, b, e = lax.axis_index("trip"), lax.axis_index("sub"), lax.axis_index("edge")
    other = lax.rem(b + 1, ns)
    me = a * ns + b

    rest = pl.ds(1, layers - 1)
    loads = [
        pltpu.make_async_copy(s, d, in_sem.at[i])
        for i, (s, d) in enumerate([(feat_hbm.at[:, pl.ds(k * CHUNK, CHUNK), :], out.at[:, pl.ds(k * CHUNK, CHUNK), :]) for k in range(nk)] + [(down_hbm.at[rest], down.at[rest]), (coef_hbm, coef), (up_hbm, up), (dense_hbm, dense), (down_hbm.at[0], down.at[0])])
    ]
    l_down, l_coef, l_up, l_dense, l_first = range(nk, nk + 5)
    loads[l_first].start()
    for k in range(nk):
        loads[k].start()

    barrier = pltpu.get_barrier_semaphore()
    for o in range(1, nt):
        pl.semaphore_signal(barrier, inc=1, device_id={"trip": lax.rem(a + o, nt)}, device_id_type=MESH)
    pl.semaphore_signal(barrier, inc=1, device_id={"sub": other}, device_id_type=MESH)
    for o in range(1, ne):
        pl.semaphore_signal(barrier, inc=1, device_id={"edge": lax.rem(e + o, ne)}, device_id_type=MESH)

    def rows(k):
        return pl.ds(k * CHUNK, CHUNK)

    def cols(h):
        return pl.ds(h * wide, wide)

    def remote(src, dst, send, recv, where):
        return pltpu.make_async_remote_copy(
            src_ref=src, dst_ref=dst, send_sem=send, recv_sem=recv, device_id=where, device_id_type=MESH
        )

    def finished(k):
        return pltpu.make_async_copy(out.at[:, rows(k), :], out_hbm.at[:, rows(k), :], out_sem.at[k])

    def trip(o):
        return lax.rem(a + o, nt)

    def gather_piece(rank, k, h):
        return gath.at[rank, :, rows(k), cols(h)]

    def ag_far(k, h, o):
        g = gather_piece(me, k, h)
        return remote(g, g, agx_s.at[2 * k + h, o], ag_r.at[2 * k + h, me], {"trip": trip(o)})

    def ag_pair(k, h):
        g = gather_piece(me, k, h)
        return remote(g, g, agp_s.at[2 * k + h], ag_r.at[2 * k + h, me], {"sub": other})

    def ag_forward(k, h, o):
        rank = trip(o) * ns + b
        g = gather_piece(rank, k, h)
        return remote(g, g, agf_s.at[2 * k + h, o], ag_r.at[2 * k + h, rank], {"sub": other})

    def ag_arrive(k, h, rank):
        g = gather_piece(rank, k, h)
        remote(g, g, agp_s.at[2 * k + h], ag_r.at[2 * k + h, rank], {"sub": other}).wait_recv()

    def ag_send(k, h):
        for o in range(1, nt):
            ag_far(k, h, o).start()
        ag_pair(k, h).start()

    def pass_on(k, h):
        for o in range(1, nt):
            ag_arrive(k, h, trip(o) * ns + b)
            ag_forward(k, h, o).start()

    def ag_finish(h):
        for k in range(nk):
            ag_pair(k, h).wait_send()
            for o in range(1, nt):
                ag_far(k, h, o).wait_send()
                ag_forward(k, h, o).wait_send()

    def rs_pair(k, h):
        return remote(
            part.at[1, :, :, rows(k), cols(h)],
            recv1.at[:, :, rows(k), cols(h)],
            r1_s.at[2 * k + h],
            r1_r.at[2 * k + h],
            {"sub": other},
        )

    def rs_cross(k, h, o):
        return remote(
            part.at[0, o, :, rows(k), cols(h)],
            recv2.at[a, :, rows(k), cols(h)],
            r2_s.at[2 * k + h, o],
            r2_r.at[2 * k + h, a],
            {"trip": trip(o)},
        )

    def rs_arrive(k, h, o):
        src = trip(o)
        dst = recv2.at[src, :, rows(k), cols(h)]
        remote(dst, dst, r2_s.at[2 * k + h, o], r2_r.at[2 * k + h, src], {"trip": src}).wait_recv()

    def z_copy(k, h, o):
        peer = lax.rem(e + o, ne)
        return remote(
            zs.at[pl.ds(peer * cap, cap), rows(k), cols(h)],
            zr[2 * k + h].at[pl.ds(e * cap, cap)],
            z_s.at[2 * k + h, o],
            z_r.at[2 * k + h, e],
            {"edge": peer},
        )

    def z_arrive(k, h, o):
        src = lax.rem(e + o, ne)
        dst = zr[2 * k + h].at[pl.ds(src * cap, cap)]
        remote(dst, dst, z_s.at[2 * k + h, o], z_r.at[2 * k + h, src], {"edge": src}).wait_recv()

    def lower(k, layer):
        f = out[:, rows(k), :].reshape(eb * CHUNK, de)
        live = jnp.concatenate([mask[k]] * (ft // 128), axis=1)
        low = mm3(f, down_h[layer], down_l[layer]) * live
        gath[me, :, rows(k), :] = low.reshape(eb, CHUNK, ft)

    for k in range(nk):
        ids = me * r + k * CHUNK + lax.broadcasted_iota(jnp.int32, (CHUNK, 128), 0)
        for c in range(eb):
            mask[k, c * CHUNK : (c + 1) * CHUNK, :] = jnp.where(ids < counts[c], 1.0, 0.0).astype(F32)
    loads[l_first].wait()
    for i in (l_coef, l_up, l_dense, l_down):
        loads[i].start()

    def split_down(i, _):
        hi, lo = split(down[i])
        down_h[i] = hi
        down_l[i] = lo
        return 0

    split_down(0, 0)
    for k in range(nk):
        loads[k].wait()
        lower(k, 0)
        if k == 0:
            pl.semaphore_wait(barrier, nt - 1 + 1 + ne - 1)
        ag_send(k, 0)
    for k in range(nk):
        ag_send(k, 1)
    build_tables(dims, e, live_slots, pattern, rev, table)
    to_scalar = pltpu.make_async_copy(table, tab, tab_sem)
    to_scalar.start()
    loads[l_coef].wait()

    def split_coef(p, _):
        hi, lo = split(coef[p])
        c2[p, :, 0:blk] = hi
        c2[p, :, blk : 2 * blk] = lo
        return 0

    lax.fori_loop(0, slots, split_coef, 0)
    for i in (l_up, l_dense, l_down):
        loads[i].wait()
    lax.fori_loop(1, layers, split_down, 0)

    def split_rest(i, _):
        hi, lo = split(up[i])
        up_h[i] = hi
        up_l[i] = lo
        hi, lo = split(dense[i])
        dense_h[i] = hi
        dense_l[i] = lo
        return 0

    lax.fori_loop(0, layers, split_rest, 0)
    to_scalar.wait()
    for k in range(early):
        pass_on(k, 0)

    def layer_step(layer, _):
        def widen(h, pair):
            first = 2 * pair * CHUNK

            def step(c, _):
                for rank in range(ranks):
                    hi, lo = split(gath[rank, c, first : first + 2 * CHUNK, cols(h)])
                    at = rank * r + first
                    x2[h, c, at : at + 2 * CHUNK, 0:wide] = hi
                    x2[h, c, at : at + 2 * CHUNK, wide : 2 * wide] = lo
                return 0

            for k in (2 * pair, 2 * pair + 1):
                ag_arrive(k, h, a * ns + other)
                for o in range(1, nt):
                    ag_arrive(k, h, trip(o) * ns + other)
            lax.fori_loop(0, eb, step, 0, unroll=eb)

        unroll = slots

        def triplets(h):
            def step(i, prev):
                for u in range(unroll):
                    p = i * unroll + u
                    keep = tab[2, p].astype(F32)
                    w = x2[h, tab[1, p]]
                    both = dot(c2[tab[0, p]], jnp.concatenate([w, w], axis=0))
                    prev = prev * keep + (both[:, 0:wide] + both[:, wide : 2 * wide])
                    run[p] = prev
                return prev

            lax.fori_loop(0, slots // unroll, step, jnp.zeros((blk, wide), F32))

        def gather_terms(k, h):
            def collect(t, _):
                at, has = tab[3, t], tab[4, t].astype(F32)
                for o in range(nt):
                    for i in range(ns):
                        s = b if i == 0 else other
                        first = pl.multiple_of((trip(o) * ns + s) * r + k * CHUNK, CHUNK)
                        part[i, o, t, rows(k), cols(h)] = run[at, pl.ds(first, CHUNK), :] * has
                return 0

            lax.fori_loop(0, eb, collect, 0, unroll=eb)
            rs_pair(k, h).start()

        def cross(k, h):
            rs_pair(k, h).wait_recv()
            for o in range(1, nt):
                part[0, o, :, rows(k), cols(h)] = part[0, o, :, rows(k), cols(h)] + recv1[o, :, rows(k), cols(h)]
                rs_cross(k, h, o).start()
            agg[:, rows(k), cols(h)] = part[0, 0, :, rows(k), cols(h)] + recv1[0, :, rows(k), cols(h)]

        def exchange(k, h):
            total = agg[:, rows(k), cols(h)]
            for o in range(1, nt):
                rs_arrive(k, h, o)
                total = total + recv2[trip(o), :, rows(k), cols(h)]
            agg[:, rows(k), cols(h)] = total
            for o in range(1, ne):
                base = lax.rem(e + o, ne) * cap
                for s in range(cap):
                    zs[base + s, rows(k), cols(h)] = agg[tab[5, base + s], rows(k), cols(h)]
                z_copy(k, h, o).start()

        for k in range(early, nk - 1):
            pass_on(k, 0)
        @pl.when(layer > 0)
        def _():
            for k in range(nk - 1):
                pass_on(k, 1)

        for pair in range(nk // 2):
            if pair == nk // 2 - 1:
                pass_on(nk - 1, 0)
            widen(0, pair)
        triplets(0)
        gather_terms(0, 0)
        gather_terms(1, 0)

        @pl.when(layer == 0)
        def _():
            for k in range(nk - 1):
                pass_on(k, 1)

        pass_on(nk - 1, 1)
        cross(0, 0)
        cross(1, 0)
        for k in range(2, nk):
            gather_terms(k, 0)
        for pair in range(nk // 2):
            widen(1, pair)
        triplets(1)

        @pl.when(layer > 0)
        def _():
            pl.semaphore_wait(z_free, ne - 1)

        exchange(0, 0)
        ag_finish(0)
        ag_finish(1)
        gather_terms(0, 1)
        gather_terms(1, 1)
        exchange(1, 0)
        for k in range(2, nk):
            gather_terms(k, 1)
        cross(0, 1)
        cross(1, 1)
        for k in range(2, nk):
            cross(k, 0)
            cross(k, 1)
        exchange(0, 1)
        exchange(1, 1)
        for k in range(2, nk):
            exchange(k, 0)
            exchange(k, 1)
        for k in range(nk):
            sides = []
            for h in range(2):
                for o in range(1, ne):
                    z_arrive(k, h, o)
                sides.append(
                    jnp.concatenate(
                        [agg[c, rows(k), cols(h)] + zr[2 * k + h][tab[6, c]] for c in range(eb)], axis=0
                    )
                )
            both = jnp.concatenate(sides, axis=1)
            lifted = mm3(both, up_h[layer], up_l[layer])
            f = out[:, rows(k), :].reshape(eb * CHUNK, de)
            mixed = (f + lifted) * INV_THREE
            v = mm3(mixed, dense_h[layer], dense_l[layer])
            new = (mixed + v / (1.0 + jnp.exp(-v))) * jnp.where(layer + 1 < layers, INV_TWO, 1.0)
            out[:, rows(k), :] = new.reshape(eb, CHUNK, de)

            @pl.when(layer + 1 == layers)
            def _():
                finished(k).start()

            @pl.when(layer + 1 < layers)
            def _():
                lower(k, layer + 1)
                ag_send(k, 0)
                ag_send(k, 1)
                if 2 <= k < early + 2:
                    pass_on(k - 2, 0)

        @pl.when(layer + 1 < layers)
        def _():
            for o in range(1, ne):
                pl.semaphore_signal(z_free, inc=1, device_id={"edge": lax.rem(e + o, ne)}, device_id_type=MESH)

        for k in range(nk):
            for h in range(2):
                rs_pair(k, h).wait_send()
                for o in range(1, nt):
                    rs_cross(k, h, o).wait_send()
                for o in range(1, ne):
                    z_copy(k, h, o).wait_send()
        return 0

    lax.fori_loop(0, layers, layer_step, 0)
    for k in range(nk):
        finished(k).wait()


def local(edge_feat, edge_counts, reverse, patterns, trip_count, coef, down_weight, up_weight, dense_weight):
    eb, r, de = edge_feat.shape
    nt, ns, ne = lax.axis_size("trip"), lax.axis_size("sub"), lax.axis_size("edge")
    layers, _, ft = down_weight.shape
    _, _, slots, blk, _ = coef.shape
    nk, ranks = r // CHUNK, nt * ns
    cap = 2 * ((eb // 2 + ne // 2 - 1) // (ne // 2))
    dims = (nt, ns, ne, eb, r, cap, slots, layers, blk, ft, de)
    vm = pltpu.VMEM
    dma = pltpu.SemaphoreType.DMA
    scratch = [vm((ne * cap, CHUNK, ft // 2), F32) for _ in range(2 * nk)] + [
        vm(edge_feat.shape, F32),
        vm((slots, blk, blk), F32),
        vm(down_weight.shape, F32),
        vm(up_weight.shape, F32),
        vm(dense_weight.shape, F32),
        vm(down_weight.shape, BF16),
        vm(down_weight.shape, BF16),
        vm(up_weight.shape, BF16),
        vm(up_weight.shape, BF16),
        vm(dense_weight.shape, BF16),
        vm(dense_weight.shape, BF16),
        vm((slots, blk, 2 * blk), BF16),
        vm((2, eb, blk, ft), BF16),
        vm((slots, blk, ft // 2), F32),
        vm((ns, nt, eb, r, ft), F32),
        vm((nt, eb, r, ft), F32),
        vm((nt, eb, r, ft), F32),
        vm((eb, r, ft), F32),
        vm((ne * cap, r, ft), F32),
        vm((ranks, eb, r, ft), F32),
        vm((nk, eb * CHUNK, 128), F32),
        vm((8, max(128, ne * eb, slots)), jnp.int32),
        pltpu.SMEM((8, max(128, ne * eb, slots)), jnp.int32),
        dma,
        dma((nk,)),
        dma((nk + 5,)),
        dma((2 * nk, nt)),
        dma((2 * nk,)),
        dma((2 * nk, nt)),
        dma((2 * nk, ranks)),
        dma((2 * nk,)),
        dma((2 * nk,)),
        dma((2 * nk, nt)),
        dma((2 * nk, nt)),
        dma((2 * nk, ne)),
        dma((2 * nk, ne)),
        pltpu.SemaphoreType.REGULAR,
    ]
    anywhere = pl.BlockSpec(memory_space=pl.ANY)
    unscaled = pl.pallas_call(
        functools.partial(kernel, dims),
        out_shape=jax.ShapeDtypeStruct(edge_feat.shape, F32),
        in_specs=[pl.BlockSpec(memory_space=pltpu.SMEM)] + [pl.BlockSpec(memory_space=pltpu.VMEM)] * 3 + [anywhere] * 5,
        out_specs=anywhere,
        scratch_shapes=scratch,
        compiler_params=pltpu.CompilerParams(collective_id=0, has_side_effects=True, vmem_limit_bytes=64 * 1024 * 1024 - 65536),
    )(edge_counts, trip_count, patterns[0, 0].T, reverse[None, :], edge_feat, coef[0, 0], down_weight, up_weight, dense_weight)
    return unscaled * INV_TWO


def solution(mesh):
    placed = (
        P(("groups", "edge"), ("trip", "sub"), None),
        P(("groups", "edge")),
        P("groups"),
        P(("groups", "edge"), ("trip", "sub"), None, None),
        P(("groups", "edge"), ("trip", "sub")),
        P(("groups", "edge"), ("trip", "sub"), None, None, None),
        P(),
        P(),
        P(),
    )
    return jax.shard_map(
        local,
        mesh=mesh,
        in_specs=placed,
        out_specs=P(("groups", "edge"), ("trip", "sub"), None),
        check_vma=False,
    )
```
